1024 devices in a mesh: seq: 64 (over z, y), head: 16 (over x, core).
Axes of the slice: x: 8, y: 8, z: 8, core: 2. Of those that a mesh axis runs over, the one named last changes fastest.
Arguments:
- queries: bfloat16 [32768, 6144], P('seq', 'head'), may hold values from -6 to 6
- keys: bfloat16 [32768, 6144], P('seq', 'head'), may hold values from -6 to 6
- values: bfloat16 [32768, 6144], P('seq', 'head'), may hold values from -6 to 6
- attn_out: bfloat16 [32768, 6144], P('seq', 'head'), may hold values from -120 to 120
- out_grad: bfloat16 [32768, 6144], P('seq', 'head'), may hold values from -6 to 6
- norm_gain: float32 [6144], P('head'), may hold values from 0.5 to 2
Outputs:
- query_grad: bfloat16 [32768, 6144], P('seq', 'head')
- key_grad: bfloat16 [32768, 6144], P('seq', 'head')
- value_grad: bfloat16 [32768, 6144], P('seq', 'head')
The draws below stay inside these ranges and needn't reach their ends.
All inputs are finite; a program needn't handle non-finite values.
Results may differ from the reference program's by a relative error of at most 0.0057.
Values sent between devices are 32-bit elements; how exact they have to be, the bound alone decides.
No kernel may reach another device: no remote copies, remote signals or barrier semaphores. Data moves between devices by JAX's collectives and lax.ppermute only.
A program may use at most 64 MiB of HBM per device.

```python
import math
import jax
import jax.numpy as jnp
from jax import lax

D = 6144
HEADS = 48
DH = 128
GROUP = 256
TOKENS = 32768


def draw_attn_out(key, part):
    first, second, third = jax.random.split(key, 3)
    head_of = jnp.arange(D) // DH
    rising = 0.6 * 3.0 ** (head_of.astype(jnp.float32) / max(HEADS - 1, 1))
    column = jnp.exp(jax.random.uniform(second, (D,), minval=math.log(0.3), maxval=math.log(3.0)))
    row_scale = jnp.exp(jax.random.uniform(third, (TOKENS, 1), minval=math.log(0.4), maxval=math.log(4.0)))
    base = jnp.clip(jax.random.normal(first, (TOKENS, D)), -5.0, 5.0)
    vals = base * rising * column * row_scale
    return vals.astype(jnp.float32).astype(jnp.bfloat16)


def block_levels(rng, shape, shards, low, top_value):
    def one(dim, shards_of):
        heights = jax.random.uniform(jax.random.fold_in(jax.random.fold_in(rng, 6), dim), (shards_of,), jnp.float32, low / len(shards), top_value / len(shards))
        return jnp.repeat(jnp.exp(heights), shape[dim] // shards_of).reshape((-1,) + (1,) * (len(shape) - dim - 1))

    factor_of = one(*shards[0])
    for cut in shards[1:]:
        factor_of = factor_of * one(*cut)
    return factor_of


def centred(own_key, dims, deviation, limit, pieces=(), dtype=jnp.bfloat16):
    values = jax.random.normal(own_key, dims, jnp.float32) * deviation
    if len(pieces) > 0:
        values = block_levels(own_key, dims, pieces, -0.22, 0.18) * values
    return jnp.clip(values, min=-limit, max=limit).astype(dtype)


def setup_inputs(seed: int = 0) -> dict:
    key_of = jax.random.split(jax.random.key(seed), 7)
    return {
        "queries": centred(key_of[0], (TOKENS, D), 1.0, 6.0, ((0, 64), (1, 16))),
        "keys": centred(key_of[1], (TOKENS, D), 1.0, 6.0, ((0, 64), (1, 16))),
        "values": centred(key_of[2], (TOKENS, D), 1.0, 6.0, ((0, 64), (1, 16))),
        "attn_out": draw_attn_out(jax.random.fold_in(key_of[6], 71), 0),
        "out_grad": centred(key_of[4], (TOKENS, D), 1.0, 6.0, ((0, 64), (1, 16))),
        "norm_gain": jnp.clip(jnp.exp(math.log(2.0) - 1.3862944 * jax.random.uniform(key_of[5], (D,), jnp.float32) ** block_levels(key_of[5], (D,), ((0, 16),), -0.2, 0.2)), 0.5, 2.0),
    }


EPS = 1e-06

def to_half(x):
    return lax.optimization_barrier(x.astype(jnp.bfloat16)).astype(jnp.float32)

def reference(queries, keys, values, attn_out, out_grad, norm_gain):
    outf = attn_out.astype(jnp.float32)
    scaled = norm_gain[None, :].astype(jnp.float32) * out_grad.astype(jnp.float32)
    square_sum = lax.optimization_barrier(jnp.sum(outf * outf, axis=-1))
    cross_sum = lax.optimization_barrier(jnp.sum(scaled * outf, axis=-1))
    rms = jnp.sqrt(square_sum / D + EPS)
    grad_out = (scaled / rms[:, None] - outf * (cross_sum / (D * rms ** 3))[:, None]).astype(jnp.bfloat16)
    blocks = TOKENS // GROUP
    shape = (blocks, GROUP, HEADS, DH)
    qs = queries.reshape(shape)
    ks = keys.reshape(shape)
    vs = values.reshape(shape)
    gs = grad_out.reshape(shape)
    causal = jnp.arange(GROUP)[:, None] >= jnp.arange(GROUP)[None, :]
    factor = 1.0 / math.sqrt(DH * TOKENS)

    def forward(state, items):
        qb, kb, vb, gb = [a.astype(jnp.float32) for a in items]
        prods = jnp.einsum('tnj,snj->nts', gb, vb)
        prods = to_half(jnp.where(causal[None], prods, 0.0))
        grad = jnp.einsum('nts,sni->tni', prods, kb) + jnp.einsum('tnj,nij->tni', gb, to_half(state))
        state = state + jnp.einsum('tni,tnj->nij', kb, vb)
        return (state, (grad * factor).astype(jnp.bfloat16))

    def backward(state, items):
        qb, kb, vb, gb = [a.astype(jnp.float32) for a in items]
        scores = to_half(jnp.where(causal[None], jnp.einsum('tni,sni->nts', qb, kb), 0.0))
        prods = to_half(jnp.where(causal[None], jnp.einsum('tnj,snj->nts', gb, vb), 0.0))
        half_state = to_half(state)
        kgrad = jnp.einsum('nts,tni->sni', prods, qb) + jnp.einsum('snj,nij->sni', vb, half_state)
        vgrad = jnp.einsum('nts,tnj->snj', scores, gb) + jnp.einsum('sni,nij->snj', kb, half_state)
        state = state + jnp.einsum('tni,tnj->nij', qb, gb)
        return (state, ((kgrad * factor).astype(jnp.bfloat16), (vgrad * factor).astype(jnp.bfloat16)))
    start = jnp.zeros((HEADS, DH, DH), jnp.float32)
    carry, qgrad = lax.scan(forward, start, (qs, ks, vs, gs))
    carry, pair = lax.scan(backward, start, (qs, ks, vs, gs), reverse=True)
    kgrad, vgrad = pair
    return (qgrad.reshape(TOKENS, D), kgrad.reshape(TOKENS, D), vgrad.reshape(TOKENS, D))
```

```python
import functools
import math

import jax
import jax.numpy as jnp
from jax import lax
from jax.experimental import pallas as pl
from jax.experimental.pallas import tpu as pltpu
from jax.sharding import PartitionSpec as P

DH = 128
GROUP = 256
EPS = 1e-06
F32 = jnp.float32
BF16 = jnp.bfloat16
VMEM = pl.BlockSpec(memory_space=pltpu.VMEM)


def dot(a, b, contract):
    return lax.dot_general(a, b, (contract, ((), ())), preferred_element_type=F32)


NN = ((1,), (0,))
NT = ((1,), (1,))
TN = ((0,), (0,))


def stats_kernel(out_ref, grad_ref, gain_ref, send_ref):
    tokens, width = out_ref.shape
    rows = tokens // DH
    gain = gain_ref[...].reshape(1, width)
    squares, crosses = [], []
    for r in range(rows):
        o = out_ref[pl.ds(r * DH, DH), :].astype(F32)
        s = grad_ref[pl.ds(r * DH, DH), :].astype(F32) * gain
        oo, so = o * o, s * o
        sq, cr = oo[:, :DH], so[:, :DH]
        for h in range(1, width // DH):
            sq = sq + oo[:, h * DH : (h + 1) * DH]
            cr = cr + so[:, h * DH : (h + 1) * DH]
        squares.append(jnp.sum(sq.T, axis=0, keepdims=True))
        crosses.append(jnp.sum(cr.T, axis=0, keepdims=True))
    block = jnp.concatenate(squares + crosses, axis=0)
    for copy in range(send_ref.shape[0]):
        send_ref[copy] = block


def grad_out_kernel(full_width, parts_ref, out_ref, grad_ref, gain_ref, q_ref, k_ref, v_ref,
                    g_ref, state_ref, kv0_ref, qg1_ref):
    tokens, width = out_ref.shape
    heads = width // DH
    rows = tokens // DH
    total = parts_ref[0]
    for d in range(1, parts_ref.shape[0]):
        total = total + parts_ref[d]
    inv = lax.rsqrt(total[:rows] / full_width + EPS)
    coef = total[rows:] * (inv * inv * inv) / full_width
    columns = jnp.concatenate([inv, coef], axis=0).T
    gain = gain_ref[...].reshape(1, width)
    for r in range(rows):
        here = pl.ds(r * DH, DH)
        s = grad_ref[here, :].astype(F32) * gain
        o = out_ref[here, :].astype(F32)
        g = s * columns[:, r : r + 1] - o * columns[:, rows + r : rows + r + 1]
        g_ref[here, :] = g.astype(BF16)
    half = heads * DH
    for h in range(heads):
        cols = pl.ds(h * DH, DH)
        kv, qg = [], []
        for b in range(2):
            here = pl.ds(b * GROUP, GROUP)
            kv.append(dot(k_ref[here, cols], v_ref[here, cols], TN))
            qg.append(dot(q_ref[here, cols], g_ref[here, cols], TN))
        kv0_ref[pl.ds(h * DH, DH), :] = kv[0]
        qg1_ref[pl.ds(h * DH, DH), :] = qg[1]
        state_ref[pl.ds(h * DH, DH), :] = kv[0] + kv[1]
        state_ref[pl.ds(half + h * DH, DH), :] = qg[0] + qg[1]


def scan_kernel(count, x_ref, y_ref):
    step = x_ref.shape[0] // count
    forward = lax.axis_index("seq") < count // 2

    def scan(order):
        total = jnp.zeros((step, x_ref.shape[1]), F32)
        for p in order:
            y_ref[p * step : (p + 1) * step, :] = total
            total = total + x_ref[p * step : (p + 1) * step, :]

    @pl.when(forward)
    def _():
        scan(range(count))

    @pl.when(jnp.logical_not(forward))
    def _():
        scan(range(count - 1, -1, -1))


def output_kernel(factor, carry_ref, kv0_ref, qg1_ref, q_ref, k_ref, v_ref, g_ref,
                  qgrad_ref, kgrad_ref, vgrad_ref):
    width = q_ref.shape[1]
    heads = width // DH
    half = heads * DH
    row = lax.broadcasted_iota(jnp.int32, (GROUP, GROUP), 0)
    col = lax.broadcasted_iota(jnp.int32, (GROUP, GROUP), 1)
    lower = row >= col
    upper = row <= col
    for h in range(heads):
        cols = pl.ds(h * DH, DH)
        before = carry_ref[pl.ds(h * DH, DH), :]
        after = carry_ref[pl.ds(half + h * DH, DH), :]
        for b in range(2):
            here = pl.ds(b * GROUP, GROUP)
            q, k, v, g = q_ref[here, cols], k_ref[here, cols], v_ref[here, cols], g_ref[here, cols]
            if b == 0:
                fwd = before
                bwd = after + qg1_ref[pl.ds(h * DH, DH), :]
            else:
                fwd = before + kv0_ref[pl.ds(h * DH, DH), :]
                bwd = after
            fwd, bwd = fwd.astype(BF16), bwd.astype(BF16)
            prods = jnp.where(lower, dot(g, v, NT), 0.0).astype(BF16)
            prods_t = jnp.where(upper, dot(v, g, NT), 0.0).astype(BF16)
            scores_t = jnp.where(upper, dot(k, q, NT), 0.0).astype(BF16)
            qgrad = dot(prods, k, NN) + dot(g, fwd, NT)
            kgrad = dot(prods_t, q, NN) + dot(v, bwd, NT)
            vgrad = dot(scores_t, g, NN) + dot(k, bwd, NN)
            qgrad_ref[here, cols] = (qgrad * factor).astype(BF16)
            kgrad_ref[here, cols] = (kgrad * factor).astype(BF16)
            vgrad_ref[here, cols] = (vgrad * factor).astype(BF16)


def shards(queries, keys, values, attn_out, out_grad, norm_gain):
    tokens, width = queries.shape
    n_head, n_seq = lax.axis_size("head"), lax.axis_size("seq")
    full_width = width * n_head
    factor = 1.0 / math.sqrt(DH * tokens * n_seq)
    shape = jax.ShapeDtypeStruct
    params = pltpu.CompilerParams(vmem_limit_bytes=16 << 20)
    call = functools.partial(pl.pallas_call, compiler_params=params)
    send = call(
        stats_kernel,
        in_specs=[VMEM] * 3,
        out_specs=VMEM,
        out_shape=shape((n_head, 2 * tokens // DH, DH), F32),
        name="stats",
    )(attn_out, out_grad, norm_gain)
    parts = lax.all_to_all(send, "head", 0, 0)
    g, state, kv0, qg1 = call(
        functools.partial(grad_out_kernel, full_width),
        in_specs=[VMEM] * 7,
        out_specs=[VMEM] * 4,
        out_shape=[
            shape((tokens, width), BF16),
            shape((2 * width, DH), F32),
            shape((width, DH), F32),
            shape((width, DH), F32),
        ],
        name="grad_out",
    )(parts, attn_out, out_grad, norm_gain, queries, keys, values)
    piece = 2 * width * DH // n_seq
    gathered = lax.all_to_all(state.reshape(n_seq, 1, piece), "seq", 0, 0)
    scanned = call(
        functools.partial(scan_kernel, n_seq),
        in_specs=[VMEM],
        out_specs=VMEM,
        out_shape=shape((2 * width, DH), F32),
        name="scan",
    )(gathered.reshape(2 * width, DH))
    carry = lax.all_to_all(scanned.reshape(n_seq, 1, piece), "seq", 0, 0)
    return call(
        functools.partial(output_kernel, factor),
        in_specs=[VMEM] * 7,
        out_specs=[VMEM] * 3,
        out_shape=[shape((tokens, width), BF16)] * 3,
        name="outputs",
    )(carry.reshape(2 * width, DH), kv0, qg1, queries, keys, values, g)


def solution(mesh):
    spec = P("seq", "head")
    return jax.shard_map(
        shards,
        mesh=mesh,
        in_specs=(spec,) * 5 + (P("head"),),
        out_specs=(spec,) * 3,
        check_vma=False,
    )
```

```python
import functools
import math

import jax
import jax.numpy as jnp
from jax import lax
from jax.experimental import pallas as pl
from jax.experimental.pallas import tpu as pltpu
from jax.sharding import PartitionSpec as P

DH = 128
GROUP = 256
EPS = 1e-06
F32 = jnp.float32
BF16 = jnp.bfloat16
VMEM = pl.BlockSpec(memory_space=pltpu.VMEM)
HBM = pl.BlockSpec(memory_space=pltpu.HBM)


def dot(a, b, contract):
    return lax.dot_general(a, b, (contract, ((), ())), preferred_element_type=F32)


NN = ((1,), (0,))
NT = ((1,), (1,))
TN = ((0,), (0,))


def stats_kernel(out_hbm, grad_hbm, gain_hbm, v_hbm, send_ref, out_ref, grad_ref, gain_ref, v_ref, sems, gain_sem, v_sem):
    tokens, width = out_ref.shape
    rows = tokens // DH
    copies = []
    for r in range(rows):
        here = pl.ds(r * DH, DH)
        copies.append(
            (
                pltpu.make_async_copy(out_hbm.at[here], out_ref.at[here], sems.at[0, r]),
                pltpu.make_async_copy(grad_hbm.at[here], grad_ref.at[here], sems.at[1, r]),
            )
        )
    gain_copy = pltpu.make_async_copy(gain_hbm, gain_ref, gain_sem)
    v_copy = pltpu.make_async_copy(v_hbm, v_ref, v_sem)
    gain_copy.start()
    for pair in copies:
        pair[0].start()
        pair[1].start()
    v_copy.start()
    gain_copy.wait()
    gain = gain_ref[...].reshape(1, width)
    for r in range(rows):
        copies[r][0].wait()
        copies[r][1].wait()
        o = out_ref[pl.ds(r * DH, DH), :].astype(F32)
        s = grad_ref[pl.ds(r * DH, DH), :].astype(F32) * gain
        oo, so = o * o, s * o
        sq, cr = oo[:, :DH], so[:, :DH]
        for h in range(1, width // DH):
            sq = sq + oo[:, h * DH : (h + 1) * DH]
            cr = cr + so[:, h * DH : (h + 1) * DH]
        square = jnp.sum(sq.T, axis=0, keepdims=True)
        cross = jnp.sum(cr.T, axis=0, keepdims=True)
        for copy in range(send_ref.shape[0]):
            send_ref[copy, r : r + 1, :] = square
            send_ref[copy, rows + r : rows + r + 1, :] = cross
    v_copy.wait()


def grad_out_kernel(full_width, parts_ref, out_ref, grad_ref, gain_ref, q_ref, k_ref, v_ref,
                    g_ref, state_ref, kv0_ref, qg1_ref):
    tokens, width = out_ref.shape
    heads = width // DH
    rows = tokens // DH
    total = parts_ref[0]
    for d in range(1, parts_ref.shape[0]):
        total = total + parts_ref[d]
    inv = lax.rsqrt(total[:rows] / full_width + EPS)
    coef = total[rows:] * (inv * inv * inv) / full_width
    columns = jnp.concatenate([inv, coef], axis=0).T
    gain = gain_ref[...].reshape(1, width)
    for r in range(rows):
        here = pl.ds(r * DH, DH)
        s = grad_ref[here, :].astype(F32) * gain
        o = out_ref[here, :].astype(F32)
        g = s * columns[:, r : r + 1] - o * columns[:, rows + r : rows + r + 1]
        g_ref[here, :] = g.astype(BF16)
    half = heads * DH

    def terms(a_ref, b_ref, h):
        cols = pl.ds(h * DH, DH)
        return [dot(a_ref[pl.ds(b * GROUP, GROUP), cols], b_ref[pl.ds(b * GROUP, GROUP), cols], TN) for b in range(2)]

    for h in range(heads):
        qg = terms(q_ref, g_ref, h)
        qg1_ref[pl.ds(h * DH, DH), :] = qg[1]
        state_ref[pl.ds(half + h * DH, DH), :] = qg[0] + qg[1]
    for h in range(heads):
        kv = terms(k_ref, v_ref, h)
        kv0_ref[pl.ds(h * DH, DH), :] = kv[0]
        state_ref[pl.ds(h * DH, DH), :] = kv[0] + kv[1]


def scan_kernel(count, x_ref, y_ref):
    step = x_ref.shape[0] // count
    forward = lax.axis_index("seq") < count // 2

    def scan(order):
        total = jnp.zeros((step, x_ref.shape[1]), F32)
        for p in order:
            y_ref[p * step : (p + 1) * step, :] = total
            total = total + x_ref[p * step : (p + 1) * step, :]

    @pl.when(forward)
    def _():
        scan(range(count))

    @pl.when(jnp.logical_not(forward))
    def _():
        scan(range(count - 1, -1, -1))


def output_kernel(factor, carry_ref, kv0_ref, qg1_ref, q_ref, k_ref, v_ref, g_ref,
                  qgrad_hbm, kgrad_hbm, vgrad_hbm, qgrad_ref, kgrad_ref, vgrad_ref, sems):
    copies = []
    width = q_ref.shape[1]
    heads = width // DH
    half = heads * DH
    row = lax.broadcasted_iota(jnp.int32, (GROUP, GROUP), 0)
    col = lax.broadcasted_iota(jnp.int32, (GROUP, GROUP), 1)
    lower = row >= col
    upper = row <= col
    for h in range(heads):
        cols = pl.ds(h * DH, DH)
        before = carry_ref[pl.ds(h * DH, DH), :]
        after = carry_ref[pl.ds(half + h * DH, DH), :]
        for b in range(2):
            here = pl.ds(b * GROUP, GROUP)
            q, k, v, g = q_ref[here, cols], k_ref[here, cols], v_ref[here, cols], g_ref[here, cols]
            if b == 0:
                fwd = before
                bwd = after + qg1_ref[pl.ds(h * DH, DH), :]
            else:
                fwd = before + kv0_ref[pl.ds(h * DH, DH), :]
                bwd = after
            fwd, bwd = fwd.astype(BF16), bwd.astype(BF16)
            prods = jnp.where(lower, dot(g, v, NT), 0.0).astype(BF16)
            prods_t = jnp.where(upper, dot(v, g, NT), 0.0).astype(BF16)
            scores_t = jnp.where(upper, dot(k, q, NT), 0.0).astype(BF16)
            qgrad = dot(prods, k, NN) + dot(g, fwd, NT)
            kgrad = dot(prods_t, q, NN) + dot(v, bwd, NT)
            vgrad = dot(scores_t, g, NN) + dot(k, bwd, NN)
            results = (
                (qgrad, qgrad_ref, qgrad_hbm),
                (kgrad, kgrad_ref, kgrad_hbm),
                (vgrad, vgrad_ref, vgrad_hbm),
            )
            for i, (value, ref, hbm) in enumerate(results):
                ref[here, cols] = (value * factor).astype(BF16)
                copy = pltpu.make_async_copy(ref.at[here, cols], hbm.at[here, cols], sems.at[i, b, h])
                copy.start()
                copies.append(copy)
    for copy in copies:
        copy.wait()


def shards(queries, keys, values, attn_out, out_grad, norm_gain):
    tokens, width = queries.shape
    n_head, n_seq = lax.axis_size("head"), lax.axis_size("seq")
    full_width = width * n_head
    factor = 1.0 / math.sqrt(DH * tokens * n_seq)
    shape = jax.ShapeDtypeStruct
    far = functools.partial(pltpu.with_memory_space_constraint, memory_space=pltpu.HBM)
    params = pltpu.CompilerParams(vmem_limit_bytes=16 << 20)
    call = functools.partial(pl.pallas_call, compiler_params=params)
    send, out_near, grad_near, gain_near, v_near = call(
        stats_kernel,
        in_specs=[HBM] * 4,
        out_specs=[VMEM] * 5,
        out_shape=[
            shape((n_head, 2 * tokens // DH, DH), F32),
            shape((tokens, width), BF16),
            shape((tokens, width), BF16),
            shape((width,), F32),
            shape((tokens, width), BF16),
        ],
        scratch_shapes=[
            pltpu.SemaphoreType.DMA((2, tokens // DH)),
            pltpu.SemaphoreType.DMA,
            pltpu.SemaphoreType.DMA,
        ],
        name="stats",
    )(far(attn_out), far(out_grad), far(norm_gain), far(values))
    parts = lax.all_to_all(send, "head", 0, 0)
    g, state, kv0, qg1 = call(
        functools.partial(grad_out_kernel, full_width),
        in_specs=[VMEM] * 7,
        out_specs=[VMEM] * 4,
        out_shape=[
            shape((tokens, width), BF16),
            shape((2 * width, DH), F32),
            shape((width, DH), F32),
            shape((width, DH), F32),
        ],
        name="grad_out",
    )(parts, out_near, grad_near, gain_near, queries, keys, v_near)
    piece = 2 * width * DH // n_seq
    gathered = lax.all_to_all(state.reshape(n_seq, 1, piece), "seq", 0, 0)
    scanned = call(
        functools.partial(scan_kernel, n_seq),
        in_specs=[VMEM],
        out_specs=VMEM,
        out_shape=shape((2 * width, DH), F32),
        name="scan",
    )(gathered.reshape(2 * width, DH))
    carry = lax.all_to_all(scanned.reshape(n_seq, 1, piece), "seq", 0, 0)
    return call(
        functools.partial(output_kernel, factor),
        in_specs=[VMEM] * 7,
        out_specs=[HBM] * 3,
        out_shape=[shape((tokens, width), BF16)] * 3,
        scratch_shapes=[pltpu.VMEM((tokens, width), BF16)] * 3
        + [pltpu.SemaphoreType.DMA((3, tokens // GROUP, width // DH))],
        name="outputs",
    )(carry.reshape(2 * width, DH), kv0, qg1, queries, keys, v_near, g)


def solution(mesh):
    spec = P("seq", "head")
    return jax.shard_map(
        shards,
        mesh=mesh,
        in_specs=(spec,) * 5 + (P("head"),),
        out_specs=(spec,) * 3,
        check_vma=False,
    )
```

```python
import functools
import math

import jax
import jax.numpy as jnp
from jax import lax
from jax.experimental import pallas as pl
from jax.experimental.pallas import tpu as pltpu
from jax.sharding import PartitionSpec as P

DH = 128
GROUP = 256
EPS = 1e-06
F32 = jnp.float32
BF16 = jnp.bfloat16
VMEM = pl.BlockSpec(memory_space=pltpu.VMEM)
HBM = pl.BlockSpec(memory_space=pltpu.HBM)


def dot(a, b, contract):
    return lax.dot_general(a, b, (contract, ((), ())), preferred_element_type=F32)


NN = ((1,), (0,))
NT = ((1,), (1,))
TN = ((0,), (0,))


def early():
    return lax.axis_index("seq") * 8 < lax.axis_size("seq") * 5


def within_block(q, k, v, g):
    row = lax.broadcasted_iota(jnp.int32, (GROUP, GROUP), 0)
    col = lax.broadcasted_iota(jnp.int32, (GROUP, GROUP), 1)
    prods = jnp.where(row >= col, dot(g, v, NT), 0.0).astype(BF16)
    prods_t = jnp.where(row <= col, dot(v, g, NT), 0.0).astype(BF16)
    scores_t = jnp.where(row <= col, dot(k, q, NT), 0.0).astype(BF16)
    return dot(prods, k, NN), dot(prods_t, q, NN), dot(scores_t, g, NN)


def stats_kernel(out_hbm, grad_hbm, gain_hbm, q_hbm, k_hbm, v_hbm,
                 send_ref, out_ref, grad_ref, gain_ref, q_ref, k_ref, v_ref, sems, gain_sem, later_sems):
    tokens, width = out_ref.shape
    rows = tokens // DH
    copies = []
    for r in range(rows):
        here = pl.ds(r * DH, DH)
        copies.append(
            (
                pltpu.make_async_copy(out_hbm.at[here], out_ref.at[here], sems.at[0, r]),
                pltpu.make_async_copy(grad_hbm.at[here], grad_ref.at[here], sems.at[1, r]),
            )
        )
    gain_copy = pltpu.make_async_copy(gain_hbm, gain_ref, gain_sem)
    later = [
        pltpu.make_async_copy(hbm, ref, later_sems.at[i])
        for i, (hbm, ref) in enumerate(((q_hbm, q_ref), (k_hbm, k_ref), (v_hbm, v_ref)))
    ]
    gain_copy.start()
    for pair in copies:
        pair[0].start()
        pair[1].start()
    for copy in later:
        copy.start()
    gain_copy.wait()
    gain = gain_ref[...].reshape(1, width)
    for r in range(rows):
        copies[r][0].wait()
        copies[r][1].wait()
        o = out_ref[pl.ds(r * DH, DH), :].astype(F32)
        s = grad_ref[pl.ds(r * DH, DH), :].astype(F32) * gain
        oo, so = o * o, s * o
        sq, cr = oo[:, :DH], so[:, :DH]
        for h in range(1, width // DH):
            sq = sq + oo[:, h * DH : (h + 1) * DH]
            cr = cr + so[:, h * DH : (h + 1) * DH]
        square = jnp.sum(sq.T, axis=0, keepdims=True)
        cross = jnp.sum(cr.T, axis=0, keepdims=True)
        for copy in range(send_ref.shape[0]):
            send_ref[copy, r : r + 1, :] = square
            send_ref[copy, rows + r : rows + r + 1, :] = cross
    for copy in later:
        copy.wait()


def grad_out_kernel(full_width, parts_ref, out_ref, grad_ref, gain_ref, q_ref, k_ref, v_ref,
                    g_ref, state_ref, kv0_ref, qg1_ref, inner_ref):
    tokens, width = out_ref.shape
    heads = width // DH
    rows = tokens // DH
    total = parts_ref[0]
    for d in range(1, parts_ref.shape[0]):
        total = total + parts_ref[d]
    inv = lax.rsqrt(total[:rows] / full_width + EPS)
    coef = total[rows:] * (inv * inv * inv) / full_width
    columns = jnp.concatenate([inv, coef], axis=0).T
    gain = gain_ref[...].reshape(1, width)
    for r in range(rows):
        here = pl.ds(r * DH, DH)
        s = grad_ref[here, :].astype(F32) * gain
        o = out_ref[here, :].astype(F32)
        g = s * columns[:, r : r + 1] - o * columns[:, rows + r : rows + r + 1]
        g_ref[here, :] = g.astype(BF16)
    half = heads * DH

    def terms(a_ref, b_ref, h):
        cols = pl.ds(h * DH, DH)
        return [dot(a_ref[pl.ds(b * GROUP, GROUP), cols], b_ref[pl.ds(b * GROUP, GROUP), cols], TN) for b in range(2)]

    for h in range(heads):
        qg = terms(q_ref, g_ref, h)
        qg1_ref[pl.ds(h * DH, DH), :] = qg[1]
        state_ref[pl.ds(half + h * DH, DH), :] = qg[0] + qg[1]
    for h in range(heads):
        kv = terms(k_ref, v_ref, h)
        kv0_ref[pl.ds(h * DH, DH), :] = kv[0]
        state_ref[pl.ds(h * DH, DH), :] = kv[0] + kv[1]


    @pl.when(early())
    def _():
        for h in range(heads):
            for b in range(2):
                here, cols = pl.ds(b * GROUP, GROUP), pl.ds(h * DH, DH)
                tile = [ref[here, cols] for ref in (q_ref, k_ref, v_ref, g_ref)]
                for i, value in enumerate(within_block(*tile)):
                    inner_ref[i, here, cols] = value


def scan_kernel(count, x_ref, y_ref):
    step = x_ref.shape[0] // count
    forward = lax.axis_index("seq") < count // 2

    def scan(order):
        total = jnp.zeros((step, x_ref.shape[1]), F32)
        for p in order:
            y_ref[p * step : (p + 1) * step, :] = total
            total = total + x_ref[p * step : (p + 1) * step, :]

    @pl.when(forward)
    def _():
        scan(range(count))

    @pl.when(jnp.logical_not(forward))
    def _():
        scan(range(count - 1, -1, -1))


def output_kernel(factor, carry_ref, kv0_ref, qg1_ref, q_ref, k_ref, v_ref, g_ref, inner_ref,
                  qgrad_hbm, kgrad_hbm, vgrad_hbm, qgrad_ref, kgrad_ref, vgrad_ref, sems):
    width = q_ref.shape[1]
    heads = width // DH
    half = heads * DH
    results = ((qgrad_ref, qgrad_hbm), (kgrad_ref, kgrad_hbm), (vgrad_ref, vgrad_hbm))

    def copy_of(i, b, h):
        here, cols = pl.ds(b * GROUP, GROUP), pl.ds(h * DH, DH)
        ref, hbm = results[i]
        return pltpu.make_async_copy(ref.at[here, cols], hbm.at[here, cols], sems.at[i, b, h])

    def finish(inner):
        for h in range(heads):
            cols = pl.ds(h * DH, DH)
            before = carry_ref[pl.ds(h * DH, DH), :]
            after = carry_ref[pl.ds(half + h * DH, DH), :]
            for b in range(2):
                here = pl.ds(b * GROUP, GROUP)
                q, k, v, g = q_ref[here, cols], k_ref[here, cols], v_ref[here, cols], g_ref[here, cols]
                if b == 0:
                    fwd = before
                    bwd = after + qg1_ref[pl.ds(h * DH, DH), :]
                else:
                    fwd = before + kv0_ref[pl.ds(h * DH, DH), :]
                    bwd = after
                fwd, bwd = fwd.astype(BF16), bwd.astype(BF16)
                outer = dot(g, fwd, NT), dot(v, bwd, NT), dot(k, bwd, NN)
                parts = inner(here, cols, (q, k, v, g))
                for i in range(3):
                    results[i][0][here, cols] = ((parts[i] + outer[i]) * factor).astype(BF16)
                    copy_of(i, b, h).start()

    @pl.when(early())
    def _():
        finish(lambda here, cols, tile: [inner_ref[i, here, cols] for i in range(3)])

    @pl.when(jnp.logical_not(early()))
    def _():
        finish(lambda here, cols, tile: within_block(*tile))

    for i in range(3):
        for b in range(2):
            for h in range(heads):
                copy_of(i, b, h).wait()


def shards(queries, keys, values, attn_out, out_grad, norm_gain):
    tokens, width = queries.shape
    n_head, n_seq = lax.axis_size("head"), lax.axis_size("seq")
    full_width = width * n_head
    factor = 1.0 / math.sqrt(DH * tokens * n_seq)
    shape = jax.ShapeDtypeStruct
    far = functools.partial(pltpu.with_memory_space_constraint, memory_space=pltpu.HBM)
    params = pltpu.CompilerParams(vmem_limit_bytes=16 << 20)
    call = functools.partial(pl.pallas_call, compiler_params=params)
    send, out_near, grad_near, gain_near, *near = call(
        stats_kernel,
        in_specs=[HBM] * 6,
        out_specs=[VMEM] * 7,
        out_shape=[
            shape((n_head, 2 * tokens // DH, DH), F32),
            shape((tokens, width), BF16),
            shape((tokens, width), BF16),
            shape((width,), F32),
        ]
        + [shape((tokens, width), BF16)] * 3,
        scratch_shapes=[
            pltpu.SemaphoreType.DMA((2, tokens // DH)),
            pltpu.SemaphoreType.DMA,
            pltpu.SemaphoreType.DMA((3,)),
        ],
        name="stats",
    )(*map(far, (attn_out, out_grad, norm_gain, queries, keys, values)))
    parts = lax.all_to_all(send, "head", 0, 0)
    g, state, kv0, qg1, inner = call(
        functools.partial(grad_out_kernel, full_width),
        in_specs=[VMEM] * 7,
        out_specs=[VMEM] * 5,
        out_shape=[
            shape((tokens, width), BF16),
            shape((2 * width, DH), F32),
            shape((width, DH), F32),
            shape((width, DH), F32),
            shape((3, tokens, width), F32),
        ],
        name="grad_out",
    )(parts, out_near, grad_near, gain_near, *near)
    piece = 2 * width * DH // n_seq
    gathered = lax.all_to_all(state.reshape(n_seq, 1, piece), "seq", 0, 0)
    scanned = call(
        functools.partial(scan_kernel, n_seq),
        in_specs=[VMEM],
        out_specs=VMEM,
        out_shape=shape((2 * width, DH), F32),
        name="scan",
    )(gathered.reshape(2 * width, DH))
    carry = lax.all_to_all(scanned.reshape(n_seq, 1, piece), "seq", 0, 0)
    return call(
        functools.partial(output_kernel, factor),
        in_specs=[VMEM] * 8,
        out_specs=[HBM] * 3,
        out_shape=[shape((tokens, width), BF16)] * 3,
        scratch_shapes=[pltpu.VMEM((tokens, width), BF16)] * 3
        + [pltpu.SemaphoreType.DMA((3, tokens // GROUP, width // DH))],
        name="outputs",
    )(carry.reshape(2 * width, DH), kv0, qg1, *near, g, inner)


def solution(mesh):
    spec = P("seq", "head")
    return jax.shard_map(
        shards,
        mesh=mesh,
        in_specs=(spec,) * 5 + (P("head"),),
        out_specs=(spec,) * 3,
        check_vma=False,
    )
```

```python
import functools
import math

import jax
import jax.numpy as jnp
from jax import lax
from jax.experimental import pallas as pl
from jax.experimental.pallas import tpu as pltpu
from jax.sharding import PartitionSpec as P

DH = 128
GROUP = 256
EPS = 1e-06
F32 = jnp.float32
BF16 = jnp.bfloat16
VMEM = pl.BlockSpec(memory_space=pltpu.VMEM)
HBM = pl.BlockSpec(memory_space=pltpu.HBM)


def dot(a, b, contract):
    return lax.dot_general(a, b, (contract, ((), ())), preferred_element_type=F32)


NN = ((1,), (0,))
NT = ((1,), (1,))
TN = ((0,), (0,))


def ring(count):
    return math.isqrt(count)


def segments(first, rows, step):
    at = first
    while at < first + rows:
        end = min(first + rows, (at // step + 1) * step)
        yield at // step, at % step, at - first, end - at
        at = end


def early():
    return lax.axis_index("seq") * 8 < lax.axis_size("seq") * 5


def within_block(q, k, v, g):
    row = lax.broadcasted_iota(jnp.int32, (GROUP, GROUP), 0)
    col = lax.broadcasted_iota(jnp.int32, (GROUP, GROUP), 1)
    prods = jnp.where(row >= col, dot(g, v, NT), 0.0).astype(BF16)
    prods_t = jnp.where(row <= col, dot(v, g, NT), 0.0).astype(BF16)
    scores_t = jnp.where(row <= col, dot(k, q, NT), 0.0).astype(BF16)
    return dot(prods, k, NN), dot(prods_t, q, NN), dot(scores_t, g, NN)


def stats_kernel(out_hbm, grad_hbm, gain_hbm, q_hbm, k_hbm, v_hbm,
                 send_ref, out_ref, grad_ref, gain_ref, q_ref, k_ref, v_ref, sems, gain_sem, later_sems):
    tokens, width = out_ref.shape
    rows = tokens // DH
    copies = []
    for r in range(rows):
        here = pl.ds(r * DH, DH)
        copies.append(
            (
                pltpu.make_async_copy(out_hbm.at[here], out_ref.at[here], sems.at[0, r]),
                pltpu.make_async_copy(grad_hbm.at[here], grad_ref.at[here], sems.at[1, r]),
            )
        )
    gain_copy = pltpu.make_async_copy(gain_hbm, gain_ref, gain_sem)
    later = [
        pltpu.make_async_copy(hbm, ref, later_sems.at[i])
        for i, (hbm, ref) in enumerate(((q_hbm, q_ref), (k_hbm, k_ref), (v_hbm, v_ref)))
    ]
    gain_copy.start()
    for pair in copies:
        pair[0].start()
        pair[1].start()
    for copy in later:
        copy.start()
    gain_copy.wait()
    gain = gain_ref[...].reshape(1, width)
    for r in range(rows):
        copies[r][0].wait()
        copies[r][1].wait()
        o = out_ref[pl.ds(r * DH, DH), :].astype(F32)
        s = grad_ref[pl.ds(r * DH, DH), :].astype(F32) * gain
        oo, so = o * o, s * o
        sq, cr = oo[:, :DH], so[:, :DH]
        for h in range(1, width // DH):
            sq = sq + oo[:, h * DH : (h + 1) * DH]
            cr = cr + so[:, h * DH : (h + 1) * DH]
        square = jnp.sum(sq.T, axis=0, keepdims=True)
        cross = jnp.sum(cr.T, axis=0, keepdims=True)
        for copy in range(send_ref.shape[0]):
            send_ref[copy, r : r + 1, :] = square
            send_ref[copy, rows + r : rows + r + 1, :] = cross
    for copy in later:
        copy.wait()


def grad_out_kernel(full_width, parts_ref, out_ref, grad_ref, gain_ref, q_ref, k_ref, v_ref,
                    g_ref, state_ref, kv0_ref, qg1_ref, inner_ref):
    tokens, width = out_ref.shape
    heads = width // DH
    rows = tokens // DH
    total = parts_ref[0]
    for d in range(1, parts_ref.shape[0]):
        total = total + parts_ref[d]
    inv = lax.rsqrt(total[:rows] / full_width + EPS)
    coef = total[rows:] * (inv * inv * inv) / full_width
    columns = jnp.concatenate([inv, coef], axis=0).T
    gain = gain_ref[...].reshape(1, width)
    for r in range(rows):
        here = pl.ds(r * DH, DH)
        s = grad_ref[here, :].astype(F32) * gain
        o = out_ref[here, :].astype(F32)
        g = s * columns[:, r : r + 1] - o * columns[:, rows + r : rows + r + 1]
        g_ref[here, :] = g.astype(BF16)
    step = state_ref.shape[1] // 2

    def put(value, h, offset):
        for piece, to, at, length in segments(h * DH, DH, step):
            state_ref[piece, offset + to : offset + to + length, :] = value[at : at + length]

    def terms(a_ref, b_ref, h):
        cols = pl.ds(h * DH, DH)
        return [dot(a_ref[pl.ds(b * GROUP, GROUP), cols], b_ref[pl.ds(b * GROUP, GROUP), cols], TN) for b in range(2)]

    for h in range(heads):
        qg = terms(q_ref, g_ref, h)
        qg1_ref[pl.ds(h * DH, DH), :] = qg[1]
        put(qg[0] + qg[1], h, step)
    for h in range(heads):
        kv = terms(k_ref, v_ref, h)
        kv0_ref[pl.ds(h * DH, DH), :] = kv[0]
        put(kv[0] + kv[1], h, 0)


    @pl.when(early())
    def _():
        for h in range(heads):
            for b in range(2):
                here, cols = pl.ds(b * GROUP, GROUP), pl.ds(h * DH, DH)
                tile = [ref[here, cols] for ref in (q_ref, k_ref, v_ref, g_ref)]
                for i, value in enumerate(within_block(*tile)):
                    inner_ref[i, here, cols] = value


def totals_kernel(x_ref, send_ref):
    count, both, _ = x_ref.shape
    step = both // 2
    z = lax.axis_index("seq") // count
    kv = x_ref[0, :step, :]
    qg = x_ref[0, step:, :]
    for y in range(1, count):
        kv = kv + x_ref[y, :step, :]
        qg = qg + x_ref[y, step:, :]
    for other in range(send_ref.shape[0]):
        send_ref[other] = jnp.where(other > z, kv, qg)


def sums_kernel(x_ref, rows_ref, y_ref):
    count, both, _ = x_ref.shape
    step = both // 2
    z = lax.axis_index("seq") // count
    zeros = jnp.zeros((step, x_ref.shape[2]), F32)
    kv, qg = zeros, zeros
    for other in range(rows_ref.shape[0]):
        kv = kv + jnp.where(other < z, rows_ref[other], zeros)
        qg = qg + jnp.where(other > z, rows_ref[other], zeros)
    for y in range(count):
        y_ref[y, :step, :] = kv
        kv = kv + x_ref[y, :step, :]
    for y in range(count - 1, -1, -1):
        y_ref[y, step:, :] = qg
        qg = qg + x_ref[y, step:, :]


def output_kernel(factor, carry_ref, kv0_ref, qg1_ref, q_ref, k_ref, v_ref, g_ref, inner_ref,
                  qgrad_hbm, kgrad_hbm, vgrad_hbm, qgrad_ref, kgrad_ref, vgrad_ref, sems):
    width = q_ref.shape[1]
    heads = width // DH
    step = carry_ref.shape[1] // 2
    results = ((qgrad_ref, qgrad_hbm), (kgrad_ref, kgrad_hbm), (vgrad_ref, vgrad_hbm))

    def copy_of(i, b, h):
        here, cols = pl.ds(b * GROUP, GROUP), pl.ds(h * DH, DH)
        ref, hbm = results[i]
        return pltpu.make_async_copy(ref.at[here, cols], hbm.at[here, cols], sems.at[i, b, h])

    def state(h, offset):
        runs = [
            carry_ref[piece, offset + to : offset + to + length, :]
            for piece, to, _, length in segments(h * DH, DH, step)
        ]
        return jnp.concatenate(runs, axis=0)

    def finish(inner):
        for h in range(heads):
            cols = pl.ds(h * DH, DH)
            before, after = state(h, 0), state(h, step)
            for b in range(2):
                here = pl.ds(b * GROUP, GROUP)
                q, k, v, g = q_ref[here, cols], k_ref[here, cols], v_ref[here, cols], g_ref[here, cols]
                if b == 0:
                    fwd = before
                    bwd = after + qg1_ref[pl.ds(h * DH, DH), :]
                else:
                    fwd = before + kv0_ref[pl.ds(h * DH, DH), :]
                    bwd = after
                fwd, bwd = fwd.astype(BF16), bwd.astype(BF16)
                outer = dot(g, fwd, NT), dot(v, bwd, NT), dot(k, bwd, NN)
                parts = inner(here, cols, (q, k, v, g))
                for i in range(3):
                    results[i][0][here, cols] = ((parts[i] + outer[i]) * factor).astype(BF16)
                    copy_of(i, b, h).start()

    @pl.when(early())
    def _():
        finish(lambda here, cols, tile: [inner_ref[i, here, cols] for i in range(3)])

    @pl.when(jnp.logical_not(early()))
    def _():
        finish(lambda here, cols, tile: within_block(*tile))

    for i in range(3):
        for b in range(2):
            for h in range(heads):
                copy_of(i, b, h).wait()


def shards(queries, keys, values, attn_out, out_grad, norm_gain):
    tokens, width = queries.shape
    n_head, n_seq = lax.axis_size("head"), lax.axis_size("seq")
    full_width = width * n_head
    factor = 1.0 / math.sqrt(DH * tokens * n_seq)
    shape = jax.ShapeDtypeStruct
    n_ring = ring(n_seq)
    rows = [[z * n_ring + y for y in range(n_ring)] for z in range(n_seq // n_ring)]
    columns = [list(column) for column in zip(*rows)]
    exchanged = (n_ring, 2 * width // n_ring, DH)
    far = functools.partial(pltpu.with_memory_space_constraint, memory_space=pltpu.HBM)
    params = pltpu.CompilerParams(vmem_limit_bytes=16 << 20)
    call = functools.partial(pl.pallas_call, compiler_params=params)
    send, out_near, grad_near, gain_near, *near = call(
        stats_kernel,
        in_specs=[HBM] * 6,
        out_specs=[VMEM] * 7,
        out_shape=[
            shape((n_head, 2 * tokens // DH, DH), F32),
            shape((tokens, width), BF16),
            shape((tokens, width), BF16),
            shape((width,), F32),
        ]
        + [shape((tokens, width), BF16)] * 3,
        scratch_shapes=[
            pltpu.SemaphoreType.DMA((2, tokens // DH)),
            pltpu.SemaphoreType.DMA,
            pltpu.SemaphoreType.DMA((3,)),
        ],
        name="stats",
    )(*map(far, (attn_out, out_grad, norm_gain, queries, keys, values)))
    parts = lax.all_to_all(send, "head", 0, 0)
    g, state, kv0, qg1, inner = call(
        functools.partial(grad_out_kernel, full_width),
        in_specs=[VMEM] * 7,
        out_specs=[VMEM] * 5,
        out_shape=[
            shape((tokens, width), BF16),
            shape(exchanged, F32),
            shape((width, DH), F32),
            shape((width, DH), F32),
            shape((3, tokens, width), F32),
        ],
        name="grad_out",
    )(parts, out_near, grad_near, gain_near, *near)
    gathered = lax.all_to_all(state, "seq", 0, 0, axis_index_groups=rows)
    totals = call(
        totals_kernel,
        in_specs=[VMEM],
        out_specs=VMEM,
        out_shape=shape((n_seq // n_ring, width // n_ring, DH), F32),
        name="totals",
    )(gathered)
    others = lax.all_to_all(totals, "seq", 0, 0, axis_index_groups=columns)
    sums = call(
        sums_kernel,
        in_specs=[VMEM] * 2,
        out_specs=VMEM,
        out_shape=shape(exchanged, F32),
        name="sums",
    )(gathered, others)
    carry = lax.all_to_all(sums, "seq", 0, 0, axis_index_groups=rows)
    return call(
        functools.partial(output_kernel, factor),
        in_specs=[VMEM] * 8,
        out_specs=[HBM] * 3,
        out_shape=[shape((tokens, width), BF16)] * 3,
        scratch_shapes=[pltpu.VMEM((tokens, width), BF16)] * 3
        + [pltpu.SemaphoreType.DMA((3, tokens // GROUP, width // DH))],
        name="outputs",
    )(carry, kv0, qg1, *near, g, inner)


def solution(mesh):
    spec = P("seq", "head")
    return jax.shard_map(
        shards,
        mesh=mesh,
        in_specs=(spec,) * 5 + (P("head"),),
        out_specs=(spec,) * 3,
        check_vma=False,
    )
```

```python
import functools
import math

import jax
import jax.numpy as jnp
from jax import lax
from jax.experimental import pallas as pl
from jax.experimental.pallas import tpu as pltpu
from jax.sharding import PartitionSpec as P

DH = 128
GROUP = 256
EPS = 1e-06
F32 = jnp.float32
BF16 = jnp.bfloat16
VMEM = pl.BlockSpec(memory_space=pltpu.VMEM)
HBM = pl.BlockSpec(memory_space=pltpu.HBM)


def dot(a, b, contract):
    return lax.dot_general(a, b, (contract, ((), ())), preferred_element_type=F32)


NN = ((1,), (0,))
NT = ((1,), (1,))
TN = ((0,), (0,))


def early():
    waits = lax.axis_index("seq") * 8 < lax.axis_size("seq") * 5
    return jnp.logical_or(waits, lax.rem(lax.axis_index("head"), 2) == 1)


def within_block(q, k, v, g):
    row = lax.broadcasted_iota(jnp.int32, (GROUP, GROUP), 0)
    col = lax.broadcasted_iota(jnp.int32, (GROUP, GROUP), 1)
    prods = jnp.where(row >= col, dot(g, v, NT), 0.0).astype(BF16)
    prods_t = jnp.where(row <= col, dot(v, g, NT), 0.0).astype(BF16)
    scores_t = jnp.where(row <= col, dot(k, q, NT), 0.0).astype(BF16)
    return dot(prods, k, NN), dot(prods_t, q, NN), dot(scores_t, g, NN)


def stats_kernel(out_hbm, grad_hbm, gain_hbm, q_hbm, k_hbm, v_hbm,
                 send_ref, out_ref, grad_ref, gain_ref, q_ref, k_ref, v_ref, sems, gain_sem, later_sems):
    tokens, width = out_ref.shape
    rows = tokens // DH
    copies = []
    for r in range(rows):
        here = pl.ds(r * DH, DH)
        copies.append(
            (
                pltpu.make_async_copy(out_hbm.at[here], out_ref.at[here], sems.at[0, r]),
                pltpu.make_async_copy(grad_hbm.at[here], grad_ref.at[here], sems.at[1, r]),
            )
        )
    gain_copy = pltpu.make_async_copy(gain_hbm, gain_ref, gain_sem)
    later = [
        pltpu.make_async_copy(hbm, ref, later_sems.at[i])
        for i, (hbm, ref) in enumerate(((q_hbm, q_ref), (k_hbm, k_ref), (v_hbm, v_ref)))
    ]
    gain_copy.start()
    for pair in copies:
        pair[0].start()
        pair[1].start()
    for copy in later:
        copy.start()
    gain_copy.wait()
    gain = gain_ref[...].reshape(1, width)
    for r in range(rows):
        copies[r][0].wait()
        copies[r][1].wait()
        o = out_ref[pl.ds(r * DH, DH), :].astype(F32)
        s = grad_ref[pl.ds(r * DH, DH), :].astype(F32) * gain
        oo, so = o * o, s * o
        sq, cr = oo[:, :DH], so[:, :DH]
        for h in range(1, width // DH):
            sq = sq + oo[:, h * DH : (h + 1) * DH]
            cr = cr + so[:, h * DH : (h + 1) * DH]
        square = jnp.sum(sq.T, axis=0, keepdims=True)
        cross = jnp.sum(cr.T, axis=0, keepdims=True)
        for copy in range(send_ref.shape[0]):
            send_ref[copy, r : r + 1, :] = square
            send_ref[copy, rows + r : rows + r + 1, :] = cross
    for copy in later:
        copy.wait()


def grad_out_kernel(full_width, parts_ref, out_ref, grad_ref, gain_ref, q_ref, k_ref, v_ref,
                    g_ref, state_ref, kv0_ref, qg1_ref, inner_ref):
    tokens, width = out_ref.shape
    heads = width // DH
    rows = tokens // DH
    total = parts_ref[0]
    for d in range(1, parts_ref.shape[0]):
        total = total + parts_ref[d]
    inv = lax.rsqrt(total[:rows] / full_width + EPS)
    coef = total[rows:] * (inv * inv * inv) / full_width
    columns = jnp.concatenate([inv, coef], axis=0).T
    gain = gain_ref[...].reshape(1, width)
    for r in range(rows):
        here = pl.ds(r * DH, DH)
        s = grad_ref[here, :].astype(F32) * gain
        o = out_ref[here, :].astype(F32)
        g = s * columns[:, r : r + 1] - o * columns[:, rows + r : rows + r + 1]
        g_ref[here, :] = g.astype(BF16)
    half = heads * DH

    def terms(a_ref, b_ref, h):
        cols = pl.ds(h * DH, DH)
        return [dot(a_ref[pl.ds(b * GROUP, GROUP), cols], b_ref[pl.ds(b * GROUP, GROUP), cols], TN) for b in range(2)]

    for h in range(heads):
        qg = terms(q_ref, g_ref, h)
        qg1_ref[pl.ds(h * DH, DH), :] = qg[1]
        state_ref[pl.ds(half + h * DH, DH), :] = qg[0] + qg[1]
    for h in range(heads):
        kv = terms(k_ref, v_ref, h)
        kv0_ref[pl.ds(h * DH, DH), :] = kv[0]
        state_ref[pl.ds(h * DH, DH), :] = kv[0] + kv[1]


    @pl.when(early())
    def _():
        for h in range(heads):
            for b in range(2):
                here, cols = pl.ds(b * GROUP, GROUP), pl.ds(h * DH, DH)
                tile = [ref[here, cols] for ref in (q_ref, k_ref, v_ref, g_ref)]
                for i, value in enumerate(within_block(*tile)):
                    inner_ref[i, here, cols] = value


def scan_kernel(count, x_ref, y_ref):
    step = x_ref.shape[0] // count
    forward = lax.axis_index("seq") < count // 2

    def scan(order):
        total = jnp.zeros((step, x_ref.shape[1]), F32)
        for p in order:
            y_ref[p * step : (p + 1) * step, :] = total
            total = total + x_ref[p * step : (p + 1) * step, :]

    @pl.when(forward)
    def _():
        scan(range(count))

    @pl.when(jnp.logical_not(forward))
    def _():
        scan(range(count - 1, -1, -1))


def output_kernel(factor, carry_ref, kv0_ref, qg1_ref, q_ref, k_ref, v_ref, g_ref, inner_ref,
                  qgrad_hbm, kgrad_hbm, vgrad_hbm, qgrad_ref, kgrad_ref, vgrad_ref, sems):
    width = q_ref.shape[1]
    heads = width // DH
    half = heads * DH
    results = ((qgrad_ref, qgrad_hbm), (kgrad_ref, kgrad_hbm), (vgrad_ref, vgrad_hbm))

    def copy_of(i, b, h):
        here, cols = pl.ds(b * GROUP, GROUP), pl.ds(h * DH, DH)
        ref, hbm = results[i]
        return pltpu.make_async_copy(ref.at[here, cols], hbm.at[here, cols], sems.at[i, b, h])

    def finish(inner):
        for h in range(heads):
            cols = pl.ds(h * DH, DH)
            before = carry_ref[pl.ds(h * DH, DH), :]
            after = carry_ref[pl.ds(half + h * DH, DH), :]
            for b in range(2):
                here = pl.ds(b * GROUP, GROUP)
                q, k, v, g = q_ref[here, cols], k_ref[here, cols], v_ref[here, cols], g_ref[here, cols]
                if b == 0:
                    fwd = before
                    bwd = after + qg1_ref[pl.ds(h * DH, DH), :]
                else:
                    fwd = before + kv0_ref[pl.ds(h * DH, DH), :]
                    bwd = after
                fwd, bwd = fwd.astype(BF16), bwd.astype(BF16)
                outer = dot(g, fwd, NT), dot(v, bwd, NT), dot(k, bwd, NN)
                parts = inner(here, cols, (q, k, v, g))
                for i in range(3):
                    results[i][0][here, cols] = ((parts[i] + outer[i]) * factor).astype(BF16)
                    copy_of(i, b, h).start()

    @pl.when(early())
    def _():
        finish(lambda here, cols, tile: [inner_ref[i, here, cols] for i in range(3)])

    @pl.when(jnp.logical_not(early()))
    def _():
        finish(lambda here, cols, tile: within_block(*tile))

    for i in range(3):
        for b in range(2):
            for h in range(heads):
                copy_of(i, b, h).wait()


def shards(queries, keys, values, attn_out, out_grad, norm_gain):
    tokens, width = queries.shape
    n_head, n_seq = lax.axis_size("head"), lax.axis_size("seq")
    full_width = width * n_head
    factor = 1.0 / math.sqrt(DH * tokens * n_seq)
    shape = jax.ShapeDtypeStruct
    far = functools.partial(pltpu.with_memory_space_constraint, memory_space=pltpu.HBM)
    params = pltpu.CompilerParams(vmem_limit_bytes=16 << 20)
    call = functools.partial(pl.pallas_call, compiler_params=params)
    send, out_near, grad_near, gain_near, *near = call(
        stats_kernel,
        in_specs=[HBM] * 6,
        out_specs=[VMEM] * 7,
        out_shape=[
            shape((n_head, 2 * tokens // DH, DH), F32),
            shape((tokens, width), BF16),
            shape((tokens, width), BF16),
            shape((width,), F32),
        ]
        + [shape((tokens, width), BF16)] * 3,
        scratch_shapes=[
            pltpu.SemaphoreType.DMA((2, tokens // DH)),
            pltpu.SemaphoreType.DMA,
            pltpu.SemaphoreType.DMA((3,)),
        ],
        name="stats",
    )(*map(far, (attn_out, out_grad, norm_gain, queries, keys, values)))
    parts = lax.all_to_all(send, "head", 0, 0)
    g, state, kv0, qg1, inner = call(
        functools.partial(grad_out_kernel, full_width),
        in_specs=[VMEM] * 7,
        out_specs=[VMEM] * 5,
        out_shape=[
            shape((tokens, width), BF16),
            shape((2 * width, DH), F32),
            shape((width, DH), F32),
            shape((width, DH), F32),
            shape((3, tokens, width), F32),
        ],
        name="grad_out",
    )(parts, out_near, grad_near, gain_near, *near)
    piece = 2 * width * DH // n_seq
    gathered = lax.all_to_all(state.reshape(n_seq, 1, piece), "seq", 0, 0)
    scanned = call(
        functools.partial(scan_kernel, n_seq),
        in_specs=[VMEM],
        out_specs=VMEM,
        out_shape=shape((2 * width, DH), F32),
        name="scan",
    )(gathered.reshape(2 * width, DH))
    carry = lax.all_to_all(scanned.reshape(n_seq, 1, piece), "seq", 0, 0)
    return call(
        functools.partial(output_kernel, factor),
        in_specs=[VMEM] * 8,
        out_specs=[HBM] * 3,
        out_shape=[shape((tokens, width), BF16)] * 3,
        scratch_shapes=[pltpu.VMEM((tokens, width), BF16)] * 3
        + [pltpu.SemaphoreType.DMA((3, tokens // GROUP, width // DH))],
        name="outputs",
    )(carry.reshape(2 * width, DH), kv0, qg1, *near, g, inner)


def solution(mesh):
    spec = P("seq", "head")
    return jax.shard_map(
        shards,
        mesh=mesh,
        in_specs=(spec,) * 5 + (P("head"),),
        out_specs=(spec,) * 3,
        check_vma=False,
    )
```

```python
import functools
import math

import jax
import jax.numpy as jnp
from jax import lax
from jax.experimental import pallas as pl
from jax.experimental.pallas import tpu as pltpu
from jax.sharding import PartitionSpec as P

DH = 128
GROUP = 256
EPS = 1e-06
F32 = jnp.float32
BF16 = jnp.bfloat16
VMEM = pl.BlockSpec(memory_space=pltpu.VMEM)
HBM = pl.BlockSpec(memory_space=pltpu.HBM)


def dot(a, b, contract):
    return lax.dot_general(a, b, (contract, ((), ())), preferred_element_type=F32)


NN = ((1,), (0,))
NT = ((1,), (1,))
TN = ((0,), (0,))


def early():
    return lax.axis_index("seq") * 8 < lax.axis_size("seq") * 5


def within_block(q, k, v, g):
    row = lax.broadcasted_iota(jnp.int32, (GROUP, GROUP), 0)
    col = lax.broadcasted_iota(jnp.int32, (GROUP, GROUP), 1)
    prods = jnp.where(row >= col, dot(g, v, NT), 0.0).astype(BF16)
    prods_t = jnp.where(row <= col, dot(v, g, NT), 0.0).astype(BF16)
    scores_t = jnp.where(row <= col, dot(k, q, NT), 0.0).astype(BF16)
    return dot(prods, k, NN), dot(prods_t, q, NN), dot(scores_t, g, NN)


def stats_kernel(out_hbm, grad_hbm, gain_hbm, q_hbm, k_hbm, v_hbm,
                 send_ref, out_ref, grad_ref, gain_ref, q_ref, k_ref, v_ref, sems):
    tokens, width = out_ref.shape
    rows = tokens // DH
    first = [
        pltpu.make_async_copy(out_hbm, out_ref, sems.at[0]),
        pltpu.make_async_copy(grad_hbm, grad_ref, sems.at[1]),
    ]
    first.append(pltpu.make_async_copy(gain_hbm, gain_ref, sems.at[2]))
    later = [
        pltpu.make_async_copy(hbm, ref, sems.at[3 + i])
        for i, (hbm, ref) in enumerate(((q_hbm, q_ref), (k_hbm, k_ref), (v_hbm, v_ref)))
    ]
    for copy in first:
        copy.start()
    for copy in later:
        copy.start(priority=1)
    for copy in first:
        copy.wait()
    gain = gain_ref[...].reshape(1, width)
    for r in range(rows):
        o = out_ref[pl.ds(r * DH, DH), :].astype(F32)
        s = grad_ref[pl.ds(r * DH, DH), :].astype(F32) * gain
        oo, so = o * o, s * o
        sq, cr = oo[:, :DH], so[:, :DH]
        for h in range(1, width // DH):
            sq = sq + oo[:, h * DH : (h + 1) * DH]
            cr = cr + so[:, h * DH : (h + 1) * DH]
        square = jnp.sum(sq.T, axis=0, keepdims=True)
        cross = jnp.sum(cr.T, axis=0, keepdims=True)
        for copy in range(send_ref.shape[0]):
            send_ref[copy, r : r + 1, :] = square
            send_ref[copy, rows + r : rows + r + 1, :] = cross
    for copy in later:
        copy.wait()


def grad_out_kernel(full_width, parts_ref, out_ref, grad_ref, gain_ref, q_ref, k_ref, v_ref,
                    g_ref, state_ref, kv0_ref, qg1_ref, inner_ref):
    tokens, width = out_ref.shape
    heads = width // DH
    rows = tokens // DH
    parts = [parts_ref[d] for d in range(parts_ref.shape[0])]
    while len(parts) > 1:
        parts = [a + b for a, b in zip(parts[::2], parts[1::2])]
    total = parts[0]
    inv = lax.rsqrt(total[:rows] / full_width + EPS)
    coef = total[rows:] * (inv * inv * inv) / full_width
    columns = jnp.concatenate([inv, coef], axis=0).T
    gain = gain_ref[...].reshape(1, width)
    for r in range(rows):
        here = pl.ds(r * DH, DH)
        s = grad_ref[here, :].astype(F32) * gain
        o = out_ref[here, :].astype(F32)
        g = s * columns[:, r : r + 1] - o * columns[:, rows + r : rows + r + 1]
        g_ref[here, :] = g.astype(BF16)
    half = heads * DH

    def terms(a_ref, b_ref, h):
        cols = pl.ds(h * DH, DH)
        return [dot(a_ref[pl.ds(b * GROUP, GROUP), cols], b_ref[pl.ds(b * GROUP, GROUP), cols], TN) for b in range(2)]

    for h in range(heads):
        qg = terms(q_ref, g_ref, h)
        qg1_ref[pl.ds(h * DH, DH), :] = qg[1]
        state_ref[pl.ds(half + h * DH, DH), :] = qg[0] + qg[1]
    for h in range(heads):
        kv = terms(k_ref, v_ref, h)
        kv0_ref[pl.ds(h * DH, DH), :] = kv[0]
        state_ref[pl.ds(h * DH, DH), :] = kv[0] + kv[1]


    @pl.when(early())
    def _():
        for h in range(heads):
            for b in range(2):
                here, cols = pl.ds(b * GROUP, GROUP), pl.ds(h * DH, DH)
                tile = [ref[here, cols] for ref in (q_ref, k_ref, v_ref, g_ref)]
                for i, value in enumerate(within_block(*tile)):
                    inner_ref[i, here, cols] = value


def scan_kernel(count, x_ref, y_ref):
    step = x_ref.shape[0] // count
    forward = lax.axis_index("seq") < count // 2

    def scan(order):
        total = jnp.zeros((step, x_ref.shape[1]), F32)
        for p in order:
            y_ref[p * step : (p + 1) * step, :] = total
            total = total + x_ref[p * step : (p + 1) * step, :]

    @pl.when(forward)
    def _():
        scan(range(count))

    @pl.when(jnp.logical_not(forward))
    def _():
        scan(range(count - 1, -1, -1))


def output_kernel(factor, carry_ref, kv0_ref, qg1_ref, q_ref, k_ref, v_ref, g_ref, inner_ref,
                  qgrad_hbm, kgrad_hbm, vgrad_hbm, qgrad_ref, kgrad_ref, vgrad_ref, sems):
    width = q_ref.shape[1]
    heads = width // DH
    half = heads * DH
    results = ((qgrad_ref, qgrad_hbm), (kgrad_ref, kgrad_hbm), (vgrad_ref, vgrad_hbm))

    def copy_of(i, b, h):
        here, cols = pl.ds(b * GROUP, GROUP), pl.ds(h * DH, DH)
        ref, hbm = results[i]
        return pltpu.make_async_copy(ref.at[here, cols], hbm.at[here, cols], sems.at[i, b, h])

    def finish(inner):
        for h in range(heads):
            cols = pl.ds(h * DH, DH)
            before = carry_ref[pl.ds(h * DH, DH), :]
            after = carry_ref[pl.ds(half + h * DH, DH), :]
            for b in range(2):
                here = pl.ds(b * GROUP, GROUP)
                q, k, v, g = q_ref[here, cols], k_ref[here, cols], v_ref[here, cols], g_ref[here, cols]
                if b == 0:
                    fwd = before
                    bwd = after + qg1_ref[pl.ds(h * DH, DH), :]
                else:
                    fwd = before + kv0_ref[pl.ds(h * DH, DH), :]
                    bwd = after
                fwd, bwd = fwd.astype(BF16), bwd.astype(BF16)
                outer = dot(g, fwd, NT), dot(v, bwd, NT), dot(k, bwd, NN)
                parts = inner(here, cols, (q, k, v, g))
                for i in range(3):
                    results[i][0][here, cols] = ((parts[i] + outer[i]) * factor).astype(BF16)
                    copy_of(i, b, h).start()

    @pl.when(early())
    def _():
        finish(lambda here, cols, tile: [inner_ref[i, here, cols] for i in range(3)])

    @pl.when(jnp.logical_not(early()))
    def _():
        finish(lambda here, cols, tile: within_block(*tile))

    for i in range(3):
        for b in range(2):
            for h in range(heads):
                copy_of(i, b, h).wait()


def shards(queries, keys, values, attn_out, out_grad, norm_gain):
    tokens, width = queries.shape
    n_head, n_seq = lax.axis_size("head"), lax.axis_size("seq")
    full_width = width * n_head
    factor = 1.0 / math.sqrt(DH * tokens * n_seq)
    shape = jax.ShapeDtypeStruct
    far = functools.partial(pltpu.with_memory_space_constraint, memory_space=pltpu.HBM)
    params = pltpu.CompilerParams(vmem_limit_bytes=16 << 20)
    call = functools.partial(pl.pallas_call, compiler_params=params)
    send, out_near, grad_near, gain_near, *near = call(
        stats_kernel,
        in_specs=[HBM] * 6,
        out_specs=[VMEM] * 7,
        out_shape=[
            shape((n_head, 2 * tokens // DH, DH), F32),
            shape((tokens, width), BF16),
            shape((tokens, width), BF16),
            shape((width,), F32),
        ]
        + [shape((tokens, width), BF16)] * 3,
        scratch_shapes=[pltpu.SemaphoreType.DMA((6,))],
        name="stats",
    )(*map(far, (attn_out, out_grad, norm_gain, queries, keys, values)))
    parts = lax.all_to_all(send, "head", 0, 0)
    g, state, kv0, qg1, inner = call(
        functools.partial(grad_out_kernel, full_width),
        in_specs=[VMEM] * 7,
        out_specs=[VMEM] * 5,
        out_shape=[
            shape((tokens, width), BF16),
            shape((2 * width, DH), F32),
            shape((width, DH), F32),
            shape((width, DH), F32),
            shape((3, tokens, width), F32),
        ],
        name="grad_out",
    )(parts, out_near, grad_near, gain_near, *near)
    piece = 2 * width * DH // n_seq
    gathered = lax.all_to_all(state.reshape(n_seq, 1, piece), "seq", 0, 0)
    scanned = call(
        functools.partial(scan_kernel, n_seq),
        in_specs=[VMEM],
        out_specs=VMEM,
        out_shape=shape((2 * width, DH), F32),
        name="scan",
    )(gathered.reshape(2 * width, DH))
    carry = lax.all_to_all(scanned.reshape(n_seq, 1, piece), "seq", 0, 0)
    return call(
        functools.partial(output_kernel, factor),
        in_specs=[VMEM] * 8,
        out_specs=[HBM] * 3,
        out_shape=[shape((tokens, width), BF16)] * 3,
        scratch_shapes=[pltpu.VMEM((tokens, width), BF16)] * 3
        + [pltpu.SemaphoreType.DMA((3, tokens // GROUP, width // DH))],
        name="outputs",
    )(carry.reshape(2 * width, DH), kv0, qg1, *near, g, inner)


def solution(mesh):
    spec = P("seq", "head")
    return jax.shard_map(
        shards,
        mesh=mesh,
        in_specs=(spec,) * 5 + (P("head"),),
        out_specs=(spec,) * 3,
        check_vma=False,
    )
```

```python
import functools
import math

import jax
import jax.numpy as jnp
from jax import lax
from jax.experimental import pallas as pl
from jax.experimental.pallas import tpu as pltpu
from jax.sharding import PartitionSpec as P

DH = 128
GROUP = 256
EPS = 1e-06
F32 = jnp.float32
BF16 = jnp.bfloat16
VMEM = pl.BlockSpec(memory_space=pltpu.VMEM)
HBM = pl.BlockSpec(memory_space=pltpu.HBM)


def dot(a, b, contract):
    return lax.dot_general(a, b, (contract, ((), ())), preferred_element_type=F32)


NN = ((1,), (0,))
NT = ((1,), (1,))
TN = ((0,), (0,))


def early():
    waits = lax.axis_index("seq") * 8 < lax.axis_size("seq") * 5
    return jnp.logical_or(waits, lax.rem(lax.axis_index("head"), 2) == 0)


def within_block(q, k, v, g):
    row = lax.broadcasted_iota(jnp.int32, (GROUP, GROUP), 0)
    col = lax.broadcasted_iota(jnp.int32, (GROUP, GROUP), 1)
    prods = jnp.where(row >= col, dot(g, v, NT), 0.0).astype(BF16)
    prods_t = jnp.where(row <= col, dot(v, g, NT), 0.0).astype(BF16)
    scores_t = jnp.where(row <= col, dot(k, q, NT), 0.0).astype(BF16)
    return dot(prods, k, NN), dot(prods_t, q, NN), dot(scores_t, g, NN)


def stats_kernel(out_hbm, grad_hbm, gain_hbm, q_hbm, k_hbm, v_hbm,
                 send_ref, out_ref, grad_ref, gain_ref, q_ref, k_ref, v_ref, sems):
    tokens, width = out_ref.shape
    rows = tokens // DH
    first = [
        pltpu.make_async_copy(out_hbm, out_ref, sems.at[0]),
        pltpu.make_async_copy(grad_hbm, grad_ref, sems.at[1]),
    ]
    first.append(pltpu.make_async_copy(gain_hbm, gain_ref, sems.at[2]))
    later = [
        pltpu.make_async_copy(hbm, ref, sems.at[3 + i])
        for i, (hbm, ref) in enumerate(((q_hbm, q_ref), (k_hbm, k_ref), (v_hbm, v_ref)))
    ]
    for copy in first:
        copy.start()
    for copy in later:
        copy.start(priority=1)
    for copy in first:
        copy.wait()
    gain = gain_ref[...].reshape(1, width)
    for r in range(rows):
        o = out_ref[pl.ds(r * DH, DH), :].astype(F32)
        s = grad_ref[pl.ds(r * DH, DH), :].astype(F32) * gain
        oo, so = o * o, s * o
        sq, cr = oo[:, :DH], so[:, :DH]
        for h in range(1, width // DH):
            sq = sq + oo[:, h * DH : (h + 1) * DH]
            cr = cr + so[:, h * DH : (h + 1) * DH]
        square = jnp.sum(sq.T, axis=0, keepdims=True)
        cross = jnp.sum(cr.T, axis=0, keepdims=True)
        for copy in range(send_ref.shape[0]):
            send_ref[copy, r : r + 1, :] = square
            send_ref[copy, rows + r : rows + r + 1, :] = cross
    for copy in later:
        copy.wait()


def grad_out_kernel(full_width, parts_ref, out_ref, grad_ref, gain_ref, q_ref, k_ref, v_ref,
                    g_ref, state_ref, kv0_ref, qg1_ref, inner_ref):
    tokens, width = out_ref.shape
    heads = width // DH
    rows = tokens // DH
    parts = [parts_ref[d] for d in range(parts_ref.shape[0])]
    while len(parts) > 1:
        parts = [a + b for a, b in zip(parts[::2], parts[1::2])]
    total = parts[0]
    inv = lax.rsqrt(total[:rows] / full_width + EPS)
    coef = total[rows:] * (inv * inv * inv) / full_width
    columns = jnp.concatenate([inv, coef], axis=0).T
    gain = gain_ref[...].reshape(1, width)
    for r in range(rows):
        here = pl.ds(r * DH, DH)
        s = grad_ref[here, :].astype(F32) * gain
        o = out_ref[here, :].astype(F32)
        g = s * columns[:, r : r + 1] - o * columns[:, rows + r : rows + r + 1]
        g_ref[here, :] = g.astype(BF16)
    half = heads * DH

    def terms(a_ref, b_ref, h):
        cols = pl.ds(h * DH, DH)
        return [dot(a_ref[pl.ds(b * GROUP, GROUP), cols], b_ref[pl.ds(b * GROUP, GROUP), cols], TN) for b in range(2)]

    for h in range(heads):
        qg = terms(q_ref, g_ref, h)
        qg1_ref[pl.ds(h * DH, DH), :] = qg[1]
        state_ref[pl.ds(half + h * DH, DH), :] = qg[0] + qg[1]
    for h in range(heads):
        kv = terms(k_ref, v_ref, h)
        kv0_ref[pl.ds(h * DH, DH), :] = kv[0]
        state_ref[pl.ds(h * DH, DH), :] = kv[0] + kv[1]


    @pl.when(early())
    def _():
        for h in range(heads):
            for b in range(2):
                here, cols = pl.ds(b * GROUP, GROUP), pl.ds(h * DH, DH)
                tile = [ref[here, cols] for ref in (q_ref, k_ref, v_ref, g_ref)]
                for i, value in enumerate(within_block(*tile)):
                    inner_ref[i, here, cols] = value


def scan_kernel(count, x_ref, y_ref):
    step = x_ref.shape[0] // count
    forward = lax.axis_index("seq") < count // 2

    def scan(order):
        total = jnp.zeros((step, x_ref.shape[1]), F32)
        for p in order:
            y_ref[p * step : (p + 1) * step, :] = total
            total = total + x_ref[p * step : (p + 1) * step, :]

    @pl.when(forward)
    def _():
        scan(range(count))

    @pl.when(jnp.logical_not(forward))
    def _():
        scan(range(count - 1, -1, -1))


def output_kernel(factor, carry_ref, kv0_ref, qg1_ref, q_ref, k_ref, v_ref, g_ref, inner_ref,
                  qgrad_hbm, kgrad_hbm, vgrad_hbm, qgrad_ref, kgrad_ref, vgrad_ref, sems):
    width = q_ref.shape[1]
    heads = width // DH
    half = heads * DH
    results = ((qgrad_ref, qgrad_hbm), (kgrad_ref, kgrad_hbm), (vgrad_ref, vgrad_hbm))

    def copy_of(i, b, h):
        here, cols = pl.ds(b * GROUP, GROUP), pl.ds(h * DH, DH)
        ref, hbm = results[i]
        return pltpu.make_async_copy(ref.at[here, cols], hbm.at[here, cols], sems.at[i, b, h])

    def finish(inner):
        for h in range(heads):
            cols = pl.ds(h * DH, DH)
            before = carry_ref[pl.ds(h * DH, DH), :]
            after = carry_ref[pl.ds(half + h * DH, DH), :]
            for b in range(2):
                here = pl.ds(b * GROUP, GROUP)
                q, k, v, g = q_ref[here, cols], k_ref[here, cols], v_ref[here, cols], g_ref[here, cols]
                if b == 0:
                    fwd = before
                    bwd = after + qg1_ref[pl.ds(h * DH, DH), :]
                else:
                    fwd = before + kv0_ref[pl.ds(h * DH, DH), :]
                    bwd = after
                fwd, bwd = fwd.astype(BF16), bwd.astype(BF16)
                outer = dot(g, fwd, NT), dot(v, bwd, NT), dot(k, bwd, NN)
                parts = inner(here, cols, (q, k, v, g))
                for i in range(3):
                    results[i][0][here, cols] = ((parts[i] + outer[i]) * factor).astype(BF16)
                    copy_of(i, b, h).start()

    @pl.when(early())
    def _():
        finish(lambda here, cols, tile: [inner_ref[i, here, cols] for i in range(3)])

    @pl.when(jnp.logical_not(early()))
    def _():
        finish(lambda here, cols, tile: within_block(*tile))

    for i in range(3):
        for b in range(2):
            for h in range(heads):
                copy_of(i, b, h).wait()


def shards(queries, keys, values, attn_out, out_grad, norm_gain):
    tokens, width = queries.shape
    n_head, n_seq = lax.axis_size("head"), lax.axis_size("seq")
    full_width = width * n_head
    factor = 1.0 / math.sqrt(DH * tokens * n_seq)
    shape = jax.ShapeDtypeStruct
    far = functools.partial(pltpu.with_memory_space_constraint, memory_space=pltpu.HBM)
    params = pltpu.CompilerParams(vmem_limit_bytes=16 << 20)
    call = functools.partial(pl.pallas_call, compiler_params=params)
    send, out_near, grad_near, gain_near, *near = call(
        stats_kernel,
        in_specs=[HBM] * 6,
        out_specs=[VMEM] * 7,
        out_shape=[
            shape((n_head, 2 * tokens // DH, DH), F32),
            shape((tokens, width), BF16),
            shape((tokens, width), BF16),
            shape((width,), F32),
        ]
        + [shape((tokens, width), BF16)] * 3,
        scratch_shapes=[pltpu.SemaphoreType.DMA((6,))],
        name="stats",
    )(*map(far, (attn_out, out_grad, norm_gain, queries, keys, values)))
    parts = lax.all_to_all(send, "head", 0, 0)
    g, state, kv0, qg1, inner = call(
        functools.partial(grad_out_kernel, full_width),
        in_specs=[VMEM] * 7,
        out_specs=[VMEM] * 5,
        out_shape=[
            shape((tokens, width), BF16),
            shape((2 * width, DH), F32),
            shape((width, DH), F32),
            shape((width, DH), F32),
            shape((3, tokens, width), F32),
        ],
        name="grad_out",
    )(parts, out_near, grad_near, gain_near, *near)
    piece = 2 * width * DH // n_seq
    gathered = lax.all_to_all(state.reshape(n_seq, 1, piece), "seq", 0, 0)
    scanned = call(
        functools.partial(scan_kernel, n_seq),
        in_specs=[VMEM],
        out_specs=VMEM,
        out_shape=shape((2 * width, DH), F32),
        name="scan",
    )(gathered.reshape(2 * width, DH))
    carry = lax.all_to_all(scanned.reshape(n_seq, 1, piece), "seq", 0, 0)
    return call(
        functools.partial(output_kernel, factor),
        in_specs=[VMEM] * 8,
        out_specs=[HBM] * 3,
        out_shape=[shape((tokens, width), BF16)] * 3,
        scratch_shapes=[pltpu.VMEM((tokens, width), BF16)] * 3
        + [pltpu.SemaphoreType.DMA((3, tokens // GROUP, width // DH))],
        name="outputs",
    )(carry.reshape(2 * width, DH), kv0, qg1, *near, g, inner)


def solution(mesh):
    spec = P("seq", "head")
    return jax.shard_map(
        shards,
        mesh=mesh,
        in_specs=(spec,) * 5 + (P("head"),),
        out_specs=(spec,) * 3,
        check_vma=False,
    )
```

```python
import functools
import math

import jax
import jax.numpy as jnp
from jax import lax
from jax.experimental import pallas as pl
from jax.experimental.pallas import tpu as pltpu
from jax.sharding import PartitionSpec as P

DH = 128
GROUP = 256
EPS = 1e-06
F32 = jnp.float32
BF16 = jnp.bfloat16
VMEM = pl.BlockSpec(memory_space=pltpu.VMEM)
HBM = pl.BlockSpec(memory_space=pltpu.HBM)


def dot(a, b, contract):
    return lax.dot_general(a, b, (contract, ((), ())), preferred_element_type=F32)


NN = ((1,), (0,))
NT = ((1,), (1,))
TN = ((0,), (0,))


def ring(count):
    return math.isqrt(count)


def segments(first, rows, step):
    at = first
    while at < first + rows:
        end = min(first + rows, (at // step + 1) * step)
        yield at // step, at % step, at - first, end - at
        at = end


def early():
    waits = lax.axis_index("seq") * 8 < lax.axis_size("seq") * 5
    return jnp.logical_or(waits, lax.rem(lax.axis_index("head"), 2) == 0)


def within_block(q, k, v, g):
    row = lax.broadcasted_iota(jnp.int32, (GROUP, GROUP), 0)
    col = lax.broadcasted_iota(jnp.int32, (GROUP, GROUP), 1)
    prods = jnp.where(row >= col, dot(g, v, NT), 0.0).astype(BF16)
    prods_t = jnp.where(row <= col, dot(v, g, NT), 0.0).astype(BF16)
    scores_t = jnp.where(row <= col, dot(k, q, NT), 0.0).astype(BF16)
    return dot(prods, k, NN), dot(prods_t, q, NN), dot(scores_t, g, NN)


def stats_kernel(out_hbm, grad_hbm, gain_hbm, q_hbm, k_hbm, v_hbm,
                 send_ref, out_ref, grad_ref, gain_ref, q_ref, k_ref, v_ref, sems):
    tokens, width = out_ref.shape
    rows = tokens // DH
    first = [
        pltpu.make_async_copy(out_hbm, out_ref, sems.at[0]),
        pltpu.make_async_copy(grad_hbm, grad_ref, sems.at[1]),
    ]
    first.append(pltpu.make_async_copy(gain_hbm, gain_ref, sems.at[2]))
    later = [
        pltpu.make_async_copy(hbm, ref, sems.at[3 + i])
        for i, (hbm, ref) in enumerate(((q_hbm, q_ref), (k_hbm, k_ref), (v_hbm, v_ref)))
    ]
    for copy in first:
        copy.start()
    for copy in later:
        copy.start(priority=1)
    for copy in first:
        copy.wait()
    gain = gain_ref[...].reshape(1, width)
    for r in range(rows):
        o = out_ref[pl.ds(r * DH, DH), :].astype(F32)
        s = grad_ref[pl.ds(r * DH, DH), :].astype(F32) * gain
        oo, so = o * o, s * o
        sq, cr = oo[:, :DH], so[:, :DH]
        for h in range(1, width // DH):
            sq = sq + oo[:, h * DH : (h + 1) * DH]
            cr = cr + so[:, h * DH : (h + 1) * DH]
        square = jnp.sum(sq.T, axis=0, keepdims=True)
        cross = jnp.sum(cr.T, axis=0, keepdims=True)
        for copy in range(send_ref.shape[0]):
            send_ref[copy, r : r + 1, :] = square
            send_ref[copy, rows + r : rows + r + 1, :] = cross
    for copy in later:
        copy.wait()


def grad_out_kernel(full_width, parts_ref, out_ref, grad_ref, gain_ref, q_ref, k_ref, v_ref,
                    g_ref, state_ref, kv0_ref, qg1_ref, inner_ref):
    tokens, width = out_ref.shape
    heads = width // DH
    rows = tokens // DH
    parts = [parts_ref[d] for d in range(parts_ref.shape[0])]
    while len(parts) > 1:
        parts = [a + b for a, b in zip(parts[::2], parts[1::2])]
    total = parts[0]
    inv = lax.rsqrt(total[:rows] / full_width + EPS)
    coef = total[rows:] * (inv * inv * inv) / full_width
    columns = jnp.concatenate([inv, coef], axis=0).T
    gain = gain_ref[...].reshape(1, width)
    for r in range(rows):
        here = pl.ds(r * DH, DH)
        s = grad_ref[here, :].astype(F32) * gain
        o = out_ref[here, :].astype(F32)
        g = s * columns[:, r : r + 1] - o * columns[:, rows + r : rows + r + 1]
        g_ref[here, :] = g.astype(BF16)
    step = state_ref.shape[1] // 2

    def put(value, h, offset):
        for piece, to, at, length in segments(h * DH, DH, step):
            state_ref[piece, offset + to : offset + to + length, :] = value[at : at + length]

    def terms(a_ref, b_ref, h):
        cols = pl.ds(h * DH, DH)
        return [dot(a_ref[pl.ds(b * GROUP, GROUP), cols], b_ref[pl.ds(b * GROUP, GROUP), cols], TN) for b in range(2)]

    for h in range(heads):
        qg = terms(q_ref, g_ref, h)
        qg1_ref[pl.ds(h * DH, DH), :] = qg[1]
        put(qg[0] + qg[1], h, step)
    for h in range(heads):
        kv = terms(k_ref, v_ref, h)
        kv0_ref[pl.ds(h * DH, DH), :] = kv[0]
        put(kv[0] + kv[1], h, 0)


    @pl.when(early())
    def _():
        for h in range(heads):
            for b in range(2):
                here, cols = pl.ds(b * GROUP, GROUP), pl.ds(h * DH, DH)
                tile = [ref[here, cols] for ref in (q_ref, k_ref, v_ref, g_ref)]
                for i, value in enumerate(within_block(*tile)):
                    inner_ref[i, here, cols] = value


def totals_kernel(x_ref, send_ref):
    count, both, _ = x_ref.shape
    step = both // 2
    z = lax.axis_index("seq") // count
    kv = x_ref[0, :step, :]
    qg = x_ref[0, step:, :]
    for y in range(1, count):
        kv = kv + x_ref[y, :step, :]
        qg = qg + x_ref[y, step:, :]
    for other in range(send_ref.shape[0]):
        send_ref[other] = jnp.where(other > z, kv, qg)


def sums_kernel(x_ref, rows_ref, y_ref):
    count, both, _ = x_ref.shape
    step = both // 2
    z = lax.axis_index("seq") // count
    zeros = jnp.zeros((step, x_ref.shape[2]), F32)
    kv, qg = zeros, zeros
    for other in range(rows_ref.shape[0]):
        kv = kv + jnp.where(other < z, rows_ref[other], zeros)
        qg = qg + jnp.where(other > z, rows_ref[other], zeros)
    for y in range(count):
        y_ref[y, :step, :] = kv
        kv = kv + x_ref[y, :step, :]
    for y in range(count - 1, -1, -1):
        y_ref[y, step:, :] = qg
        qg = qg + x_ref[y, step:, :]


def output_kernel(factor, carry_ref, kv0_ref, qg1_ref, q_ref, k_ref, v_ref, g_ref, inner_ref,
                  qgrad_hbm, kgrad_hbm, vgrad_hbm, qgrad_ref, kgrad_ref, vgrad_ref, sems):
    width = q_ref.shape[1]
    heads = width // DH
    step = carry_ref.shape[1] // 2
    results = ((qgrad_ref, qgrad_hbm), (kgrad_ref, kgrad_hbm), (vgrad_ref, vgrad_hbm))

    def copy_of(i, b, h):
        here, cols = pl.ds(b * GROUP, GROUP), pl.ds(h * DH, DH)
        ref, hbm = results[i]
        return pltpu.make_async_copy(ref.at[here, cols], hbm.at[here, cols], sems.at[i, b, h])

    def state(h, offset):
        runs = [
            carry_ref[piece, offset + to : offset + to + length, :]
            for piece, to, _, length in segments(h * DH, DH, step)
        ]
        return jnp.concatenate(runs, axis=0)

    def finish(inner):
        for h in range(heads):
            cols = pl.ds(h * DH, DH)
            before, after = state(h, 0), state(h, step)
            for b in range(2):
                here = pl.ds(b * GROUP, GROUP)
                q, k, v, g = q_ref[here, cols], k_ref[here, cols], v_ref[here, cols], g_ref[here, cols]
                if b == 0:
                    fwd = before
                    bwd = after + qg1_ref[pl.ds(h * DH, DH), :]
                else:
                    fwd = before + kv0_ref[pl.ds(h * DH, DH), :]
                    bwd = after
                fwd, bwd = fwd.astype(BF16), bwd.astype(BF16)
                outer = dot(g, fwd, NT), dot(v, bwd, NT), dot(k, bwd, NN)
                parts = inner(here, cols, (q, k, v, g))
                for i in range(3):
                    results[i][0][here, cols] = ((parts[i] + outer[i]) * factor).astype(BF16)
                    copy_of(i, b, h).start()

    @pl.when(early())
    def _():
        finish(lambda here, cols, tile: [inner_ref[i, here, cols] for i in range(3)])

    @pl.when(jnp.logical_not(early()))
    def _():
        finish(lambda here, cols, tile: within_block(*tile))

    for i in range(3):
        for b in range(2):
            for h in range(heads):
                copy_of(i, b, h).wait()


def shards(queries, keys, values, attn_out, out_grad, norm_gain):
    tokens, width = queries.shape
    n_head, n_seq = lax.axis_size("head"), lax.axis_size("seq")
    full_width = width * n_head
    factor = 1.0 / math.sqrt(DH * tokens * n_seq)
    shape = jax.ShapeDtypeStruct
    n_ring = ring(n_seq)
    rows = [[z * n_ring + y for y in range(n_ring)] for z in range(n_seq // n_ring)]
    columns = [list(column) for column in zip(*rows)]
    exchanged = (n_ring, 2 * width // n_ring, DH)
    far = functools.partial(pltpu.with_memory_space_constraint, memory_space=pltpu.HBM)
    params = pltpu.CompilerParams(vmem_limit_bytes=16 << 20)
    call = functools.partial(pl.pallas_call, compiler_params=params)
    send, out_near, grad_near, gain_near, *near = call(
        stats_kernel,
        in_specs=[HBM] * 6,
        out_specs=[VMEM] * 7,
        out_shape=[
            shape((n_head, 2 * tokens // DH, DH), F32),
            shape((tokens, width), BF16),
            shape((tokens, width), BF16),
            shape((width,), F32),
        ]
        + [shape((tokens, width), BF16)] * 3,
        scratch_shapes=[pltpu.SemaphoreType.DMA((6,))],
        name="stats",
    )(*map(far, (attn_out, out_grad, norm_gain, queries, keys, values)))
    parts = lax.all_to_all(send, "head", 0, 0)
    g, state, kv0, qg1, inner = call(
        functools.partial(grad_out_kernel, full_width),
        in_specs=[VMEM] * 7,
        out_specs=[VMEM] * 5,
        out_shape=[
            shape((tokens, width), BF16),
            shape(exchanged, F32),
            shape((width, DH), F32),
            shape((width, DH), F32),
            shape((3, tokens, width), F32),
        ],
        name="grad_out",
    )(parts, out_near, grad_near, gain_near, *near)
    gathered = lax.all_to_all(state, "seq", 0, 0, axis_index_groups=rows)
    totals = call(
        totals_kernel,
        in_specs=[VMEM],
        out_specs=VMEM,
        out_shape=shape((n_seq // n_ring, width // n_ring, DH), F32),
        name="totals",
    )(gathered)
    others = lax.all_to_all(totals, "seq", 0, 0, axis_index_groups=columns)
    sums = call(
        sums_kernel,
        in_specs=[VMEM] * 2,
        out_specs=VMEM,
        out_shape=shape(exchanged, F32),
        name="sums",
    )(gathered, others)
    carry = lax.all_to_all(sums, "seq", 0, 0, axis_index_groups=rows)
    return call(
        functools.partial(output_kernel, factor),
        in_specs=[VMEM] * 8,
        out_specs=[HBM] * 3,
        out_shape=[shape((tokens, width), BF16)] * 3,
        scratch_shapes=[pltpu.VMEM((tokens, width), BF16)] * 3
        + [pltpu.SemaphoreType.DMA((3, tokens // GROUP, width // DH))],
        name="outputs",
    )(carry, kv0, qg1, *near, g, inner)


def solution(mesh):
    spec = P("seq", "head")
    return jax.shard_map(
        shards,
        mesh=mesh,
        in_specs=(spec,) * 5 + (P("head"),),
        out_specs=(spec,) * 3,
        check_vma=False,
    )
```

```python
import functools
import math

import jax
import jax.numpy as jnp
from jax import lax
from jax.experimental import pallas as pl
from jax.experimental.pallas import tpu as pltpu
from jax.sharding import PartitionSpec as P

DH = 128
GROUP = 256
EPS = 1e-06
F32 = jnp.float32
BF16 = jnp.bfloat16
VMEM = pl.BlockSpec(memory_space=pltpu.VMEM)
HBM = pl.BlockSpec(memory_space=pltpu.HBM)


def dot(a, b, contract):
    return lax.dot_general(a, b, (contract, ((), ())), preferred_element_type=F32)


NN = ((1,), (0,))
NT = ((1,), (1,))
TN = ((0,), (0,))


def early():
    return lax.rem(lax.axis_index("head"), 2) == 0


def within_block(q, k, v, g):
    row = lax.broadcasted_iota(jnp.int32, (GROUP, GROUP), 0)
    col = lax.broadcasted_iota(jnp.int32, (GROUP, GROUP), 1)
    prods = jnp.where(row >= col, dot(g, v, NT), 0.0).astype(BF16)
    prods_t = jnp.where(row <= col, dot(v, g, NT), 0.0).astype(BF16)
    scores_t = jnp.where(row <= col, dot(k, q, NT), 0.0).astype(BF16)
    return dot(prods, k, NN), dot(prods_t, q, NN), dot(scores_t, g, NN)


def stats_kernel(out_hbm, grad_hbm, gain_hbm, q_hbm, k_hbm, v_hbm,
                 send_ref, out_ref, grad_ref, gain_ref, q_ref, k_ref, v_ref, sems):
    tokens, width = out_ref.shape
    rows = tokens // DH
    first = [
        pltpu.make_async_copy(out_hbm, out_ref, sems.at[0]),
        pltpu.make_async_copy(grad_hbm, grad_ref, sems.at[1]),
    ]
    first.append(pltpu.make_async_copy(gain_hbm, gain_ref, sems.at[2]))
    later = [
        pltpu.make_async_copy(hbm, ref, sems.at[3 + i])
        for i, (hbm, ref) in enumerate(((q_hbm, q_ref), (k_hbm, k_ref), (v_hbm, v_ref)))
    ]
    for copy in first:
        copy.start()
    for copy in later:
        copy.start(priority=1)
    for copy in first:
        copy.wait()
    gain = gain_ref[...].reshape(1, width)
    for r in range(rows):
        o = out_ref[pl.ds(r * DH, DH), :].astype(F32)
        s = grad_ref[pl.ds(r * DH, DH), :].astype(F32) * gain
        oo, so = o * o, s * o
        sq, cr = oo[:, :DH], so[:, :DH]
        for h in range(1, width // DH):
            sq = sq + oo[:, h * DH : (h + 1) * DH]
            cr = cr + so[:, h * DH : (h + 1) * DH]
        square = jnp.sum(sq.T, axis=0, keepdims=True)
        cross = jnp.sum(cr.T, axis=0, keepdims=True)
        for copy in range(send_ref.shape[0]):
            send_ref[copy, r : r + 1, :] = square
            send_ref[copy, rows + r : rows + r + 1, :] = cross
    for copy in later:
        copy.wait()


def grad_out_kernel(full_width, parts_ref, out_ref, grad_ref, gain_ref, q_ref, k_ref, v_ref,
                    g_ref, state_ref, kv0_ref, qg1_ref, inner_ref):
    tokens, width = out_ref.shape
    heads = width // DH
    rows = tokens // DH
    parts = [parts_ref[d] for d in range(parts_ref.shape[0])]
    while len(parts) > 1:
        parts = [a + b for a, b in zip(parts[::2], parts[1::2])]
    total = parts[0]
    inv = lax.rsqrt(total[:rows] / full_width + EPS)
    coef = total[rows:] * (inv * inv * inv) / full_width
    columns = jnp.concatenate([inv, coef], axis=0).T
    gain = gain_ref[...].reshape(1, width)
    for r in range(rows):
        here = pl.ds(r * DH, DH)
        s = grad_ref[here, :].astype(F32) * gain
        o = out_ref[here, :].astype(F32)
        g = s * columns[:, r : r + 1] - o * columns[:, rows + r : rows + r + 1]
        g_ref[here, :] = g.astype(BF16)
    half = heads * DH

    def terms(a_ref, b_ref, h):
        cols = pl.ds(h * DH, DH)
        return [dot(a_ref[pl.ds(b * GROUP, GROUP), cols], b_ref[pl.ds(b * GROUP, GROUP), cols], TN) for b in range(2)]

    for h in range(heads):
        qg = terms(q_ref, g_ref, h)
        qg1_ref[pl.ds(h * DH, DH), :] = qg[1]
        state_ref[pl.ds(half + h * DH, DH), :] = qg[0] + qg[1]
    for h in range(heads):
        kv = terms(k_ref, v_ref, h)
        kv0_ref[pl.ds(h * DH, DH), :] = kv[0]
        state_ref[pl.ds(h * DH, DH), :] = kv[0] + kv[1]


    @pl.when(early())
    def _():
        for h in range(heads):
            for b in range(2):
                here, cols = pl.ds(b * GROUP, GROUP), pl.ds(h * DH, DH)
                tile = [ref[here, cols] for ref in (q_ref, k_ref, v_ref, g_ref)]
                for i, value in enumerate(within_block(*tile)):
                    inner_ref[i, here, cols] = value


def scan_kernel(count, x_ref, y_ref):
    step = x_ref.shape[0] // count
    forward = lax.axis_index("seq") < count // 2

    def scan(order):
        total = jnp.zeros((step, x_ref.shape[1]), F32)
        for p in order:
            y_ref[p * step : (p + 1) * step, :] = total
            total = total + x_ref[p * step : (p + 1) * step, :]

    @pl.when(forward)
    def _():
        scan(range(count))

    @pl.when(jnp.logical_not(forward))
    def _():
        scan(range(count - 1, -1, -1))


def output_kernel(factor, carry_ref, kv0_ref, qg1_ref, q_ref, k_ref, v_ref, g_ref, inner_ref,
                  qgrad_hbm, kgrad_hbm, vgrad_hbm, qgrad_ref, kgrad_ref, vgrad_ref, sems):
    width = q_ref.shape[1]
    heads = width // DH
    half = heads * DH
    results = ((qgrad_ref, qgrad_hbm), (kgrad_ref, kgrad_hbm), (vgrad_ref, vgrad_hbm))

    def copy_of(i, b, h):
        here, cols = pl.ds(b * GROUP, GROUP), pl.ds(h * DH, DH)
        ref, hbm = results[i]
        return pltpu.make_async_copy(ref.at[here, cols], hbm.at[here, cols], sems.at[i, b, h])

    def finish(inner):
        for h in range(heads):
            cols = pl.ds(h * DH, DH)
            before = carry_ref[pl.ds(h * DH, DH), :]
            after = carry_ref[pl.ds(half + h * DH, DH), :]
            for b in range(2):
                here = pl.ds(b * GROUP, GROUP)
                q, k, v, g = q_ref[here, cols], k_ref[here, cols], v_ref[here, cols], g_ref[here, cols]
                if b == 0:
                    fwd = before
                    bwd = after + qg1_ref[pl.ds(h * DH, DH), :]
                else:
                    fwd = before + kv0_ref[pl.ds(h * DH, DH), :]
                    bwd = after
                fwd, bwd = fwd.astype(BF16), bwd.astype(BF16)
                outer = dot(g, fwd, NT), dot(v, bwd, NT), dot(k, bwd, NN)
                parts = inner(here, cols, (q, k, v, g))
                for i in range(3):
                    results[i][0][here, cols] = ((parts[i] + outer[i]) * factor).astype(BF16)
                    copy_of(i, b, h).start()

    @pl.when(early())
    def _():
        finish(lambda here, cols, tile: [inner_ref[i, here, cols] for i in range(3)])

    @pl.when(jnp.logical_not(early()))
    def _():
        finish(lambda here, cols, tile: within_block(*tile))

    for i in range(3):
        for b in range(2):
            for h in range(heads):
                copy_of(i, b, h).wait()


def shards(queries, keys, values, attn_out, out_grad, norm_gain):
    tokens, width = queries.shape
    n_head, n_seq = lax.axis_size("head"), lax.axis_size("seq")
    full_width = width * n_head
    factor = 1.0 / math.sqrt(DH * tokens * n_seq)
    shape = jax.ShapeDtypeStruct
    far = functools.partial(pltpu.with_memory_space_constraint, memory_space=pltpu.HBM)
    params = pltpu.CompilerParams(vmem_limit_bytes=16 << 20)
    call = functools.partial(pl.pallas_call, compiler_params=params)
    send, out_near, grad_near, gain_near, *near = call(
        stats_kernel,
        in_specs=[HBM] * 6,
        out_specs=[VMEM] * 7,
        out_shape=[
            shape((n_head, 2 * tokens // DH, DH), F32),
            shape((tokens, width), BF16),
            shape((tokens, width), BF16),
            shape((width,), F32),
        ]
        + [shape((tokens, width), BF16)] * 3,
        scratch_shapes=[pltpu.SemaphoreType.DMA((6,))],
        name="stats",
    )(*map(far, (attn_out, out_grad, norm_gain, queries, keys, values)))
    parts = lax.all_to_all(send, "head", 0, 0)
    g, state, kv0, qg1, inner = call(
        functools.partial(grad_out_kernel, full_width),
        in_specs=[VMEM] * 7,
        out_specs=[VMEM] * 5,
        out_shape=[
            shape((tokens, width), BF16),
            shape((2 * width, DH), F32),
            shape((width, DH), F32),
            shape((width, DH), F32),
            shape((3, tokens, width), F32),
        ],
        name="grad_out",
    )(parts, out_near, grad_near, gain_near, *near)
    piece = 2 * width * DH // n_seq
    gathered = lax.all_to_all(state.reshape(n_seq, 1, piece), "seq", 0, 0)
    scanned = call(
        functools.partial(scan_kernel, n_seq),
        in_specs=[VMEM],
        out_specs=VMEM,
        out_shape=shape((2 * width, DH), F32),
        name="scan",
    )(gathered.reshape(2 * width, DH))
    carry = lax.all_to_all(scanned.reshape(n_seq, 1, piece), "seq", 0, 0)
    return call(
        functools.partial(output_kernel, factor),
        in_specs=[VMEM] * 8,
        out_specs=[HBM] * 3,
        out_shape=[shape((tokens, width), BF16)] * 3,
        scratch_shapes=[pltpu.VMEM((tokens, width), BF16)] * 3
        + [pltpu.SemaphoreType.DMA((3, tokens // GROUP, width // DH))],
        name="outputs",
    )(carry.reshape(2 * width, DH), kv0, qg1, *near, g, inner)


def solution(mesh):
    spec = P("seq", "head")
    return jax.shard_map(
        shards,
        mesh=mesh,
        in_specs=(spec,) * 5 + (P("head"),),
        out_specs=(spec,) * 3,
        check_vma=False,
    )
```

```python
import functools
import math

import jax
import jax.numpy as jnp
from jax import lax
from jax.experimental import pallas as pl
from jax.experimental.pallas import tpu as pltpu
from jax.sharding import PartitionSpec as P

DH = 128
GROUP = 256
EPS = 1e-06
F32 = jnp.float32
BF16 = jnp.bfloat16
VMEM = pl.BlockSpec(memory_space=pltpu.VMEM)
HBM = pl.BlockSpec(memory_space=pltpu.HBM)


def dot(a, b, contract):
    return lax.dot_general(a, b, (contract, ((), ())), preferred_element_type=F32)


NN = ((1,), (0,))
NT = ((1,), (1,))
TN = ((0,), (0,))


def early():
    return lax.rem(lax.axis_index("head"), 2) == 0


def within_block(q, k, v, g):
    row = lax.broadcasted_iota(jnp.int32, (GROUP, GROUP), 0)
    col = lax.broadcasted_iota(jnp.int32, (GROUP, GROUP), 1)
    prods = jnp.where(row >= col, dot(g, v, NT), 0.0).astype(BF16)
    prods_t = jnp.where(row <= col, dot(v, g, NT), 0.0).astype(BF16)
    scores_t = jnp.where(row <= col, dot(k, q, NT), 0.0).astype(BF16)
    return dot(prods, k, NN), dot(prods_t, q, NN), dot(scores_t, g, NN)


def stats_kernel(out_hbm, grad_hbm, gain_hbm, q_hbm, k_hbm, v_hbm,
                 send_ref, out_ref, grad_ref, gain_ref, q_ref, k_ref, v_ref, sems):
    tokens, width = out_ref.shape
    rows = tokens // DH
    first = [
        pltpu.make_async_copy(out_hbm, out_ref, sems.at[0]),
        pltpu.make_async_copy(grad_hbm, grad_ref, sems.at[1]),
    ]
    first.append(pltpu.make_async_copy(gain_hbm, gain_ref, sems.at[2]))
    later = [
        pltpu.make_async_copy(hbm, ref, sems.at[3 + i])
        for i, (hbm, ref) in enumerate(((q_hbm, q_ref), (k_hbm, k_ref), (v_hbm, v_ref)))
    ]
    for copy in first:
        copy.start()
    for copy in later:
        copy.start(priority=1)
    for copy in first:
        copy.wait()
    gain = gain_ref[...].reshape(1, width)
    for r in range(rows):
        o = out_ref[pl.ds(r * DH, DH), :].astype(F32)
        s = grad_ref[pl.ds(r * DH, DH), :].astype(F32) * gain
        oo, so = o * o, s * o
        sq, cr = oo[:, :DH], so[:, :DH]
        for h in range(1, width // DH):
            sq = sq + oo[:, h * DH : (h + 1) * DH]
            cr = cr + so[:, h * DH : (h + 1) * DH]
        square = jnp.sum(sq.T, axis=0, keepdims=True)
        cross = jnp.sum(cr.T, axis=0, keepdims=True)
        for copy in range(send_ref.shape[0]):
            send_ref[copy, r : r + 1, :] = square
            send_ref[copy, rows + r : rows + r + 1, :] = cross
    for copy in later:
        copy.wait()


def grad_out_kernel(full_width, parts_ref, out_ref, grad_ref, gain_ref, q_ref, k_ref, v_ref,
                    g_ref, state_ref, kv0_ref, qg1_ref, inner_ref):
    tokens, width = out_ref.shape
    heads = width // DH
    rows = tokens // DH
    parts = [parts_ref[d] for d in range(parts_ref.shape[0])]
    while len(parts) > 1:
        parts = [a + b for a, b in zip(parts[::2], parts[1::2])]
    total = parts[0]
    inv = lax.rsqrt(total[:rows] / full_width + EPS)
    coef = total[rows:] * (inv * inv * inv) / full_width
    columns = jnp.concatenate([inv, coef], axis=0).T
    gain = gain_ref[...].reshape(1, width)
    half = heads * DH

    def term(a_ref, b_ref, b, h):
        here, cols = pl.ds(b * GROUP, GROUP), pl.ds(h * DH, DH)
        return dot(a_ref[here, cols], b_ref[here, cols], TN)

    qg = []
    for b in range(2):
        qg.append([])
        for h in range(heads):
            cols = pl.ds(h * DH, DH)
            for r in range(b * rows // 2, (b + 1) * rows // 2):
                here = pl.ds(r * DH, DH)
                s = grad_ref[here, cols].astype(F32) * gain[:, h * DH : (h + 1) * DH]
                o = out_ref[here, cols].astype(F32)
                g = s * columns[:, r : r + 1] - o * columns[:, rows + r : rows + r + 1]
                g_ref[here, cols] = g.astype(BF16)
            qg[b].append(term(q_ref, g_ref, b, h))
    for h in range(heads):
        qg1_ref[pl.ds(h * DH, DH), :] = qg[1][h]
        state_ref[pl.ds(half + h * DH, DH), :] = qg[0][h] + qg[1][h]
    for h in range(heads):
        kv = [term(k_ref, v_ref, b, h) for b in range(2)]
        kv0_ref[pl.ds(h * DH, DH), :] = kv[0]
        state_ref[pl.ds(h * DH, DH), :] = kv[0] + kv[1]

    @pl.when(early())
    def _():
        for h in range(heads):
            for b in range(2):
                here, cols = pl.ds(b * GROUP, GROUP), pl.ds(h * DH, DH)
                tile = [ref[here, cols] for ref in (q_ref, k_ref, v_ref, g_ref)]
                for i, value in enumerate(within_block(*tile)):
                    inner_ref[i, here, cols] = value


def scan_kernel(count, x_ref, y_ref):
    step = x_ref.shape[0] // count
    forward = lax.axis_index("seq") < count // 2

    def scan(order):
        total = jnp.zeros((step, x_ref.shape[1]), F32)
        for p in order:
            y_ref[p * step : (p + 1) * step, :] = total
            total = total + x_ref[p * step : (p + 1) * step, :]

    @pl.when(forward)
    def _():
        scan(range(count))

    @pl.when(jnp.logical_not(forward))
    def _():
        scan(range(count - 1, -1, -1))


def output_kernel(factor, carry_ref, kv0_ref, qg1_ref, q_ref, k_ref, v_ref, g_ref, inner_ref,
                  qgrad_hbm, kgrad_hbm, vgrad_hbm, qgrad_ref, kgrad_ref, vgrad_ref, sems):
    width = q_ref.shape[1]
    heads = width // DH
    half = heads * DH
    results = ((qgrad_ref, qgrad_hbm), (kgrad_ref, kgrad_hbm), (vgrad_ref, vgrad_hbm))

    def copy_of(i, b, h):
        here, cols = pl.ds(b * GROUP, GROUP), pl.ds(h * DH, DH)
        ref, hbm = results[i]
        return pltpu.make_async_copy(ref.at[here, cols], hbm.at[here, cols], sems.at[i, b, h])

    def finish(inner):
        for h in range(heads):
            cols = pl.ds(h * DH, DH)
            before = carry_ref[pl.ds(h * DH, DH), :]
            after = carry_ref[pl.ds(half + h * DH, DH), :]
            for b in range(2):
                here = pl.ds(b * GROUP, GROUP)
                q, k, v, g = q_ref[here, cols], k_ref[here, cols], v_ref[here, cols], g_ref[here, cols]
                if b == 0:
                    fwd = before
                    bwd = after + qg1_ref[pl.ds(h * DH, DH), :]
                else:
                    fwd = before + kv0_ref[pl.ds(h * DH, DH), :]
                    bwd = after
                fwd, bwd = fwd.astype(BF16), bwd.astype(BF16)
                outer = dot(g, fwd, NT), dot(v, bwd, NT), dot(k, bwd, NN)
                parts = inner(here, cols, (q, k, v, g))
                for i in range(3):
                    results[i][0][here, cols] = ((parts[i] + outer[i]) * factor).astype(BF16)
                    copy_of(i, b, h).start()

    @pl.when(early())
    def _():
        finish(lambda here, cols, tile: [inner_ref[i, here, cols] for i in range(3)])

    @pl.when(jnp.logical_not(early()))
    def _():
        finish(lambda here, cols, tile: within_block(*tile))

    for i in range(3):
        for b in range(2):
            for h in range(heads):
                copy_of(i, b, h).wait()


def shards(queries, keys, values, attn_out, out_grad, norm_gain):
    tokens, width = queries.shape
    n_head, n_seq = lax.axis_size("head"), lax.axis_size("seq")
    full_width = width * n_head
    factor = 1.0 / math.sqrt(DH * tokens * n_seq)
    shape = jax.ShapeDtypeStruct
    far = functools.partial(pltpu.with_memory_space_constraint, memory_space=pltpu.HBM)
    params = pltpu.CompilerParams(vmem_limit_bytes=16 << 20)
    call = functools.partial(pl.pallas_call, compiler_params=params)
    send, out_near, grad_near, gain_near, *near = call(
        stats_kernel,
        in_specs=[HBM] * 6,
        out_specs=[VMEM] * 7,
        out_shape=[
            shape((n_head, 2 * tokens // DH, DH), F32),
            shape((tokens, width), BF16),
            shape((tokens, width), BF16),
            shape((width,), F32),
        ]
        + [shape((tokens, width), BF16)] * 3,
        scratch_shapes=[pltpu.SemaphoreType.DMA((6,))],
        name="stats",
    )(*map(far, (attn_out, out_grad, norm_gain, queries, keys, values)))
    parts = lax.all_to_all(send, "head", 0, 0)
    g, state, kv0, qg1, inner = call(
        functools.partial(grad_out_kernel, full_width),
        in_specs=[VMEM] * 7,
        out_specs=[VMEM] * 5,
        out_shape=[
            shape((tokens, width), BF16),
            shape((2 * width, DH), F32),
            shape((width, DH), F32),
            shape((width, DH), F32),
            shape((3, tokens, width), F32),
        ],
        name="grad_out",
    )(parts, out_near, grad_near, gain_near, *near)
    piece = 2 * width * DH // n_seq
    gathered = lax.all_to_all(state.reshape(n_seq, 1, piece), "seq", 0, 0)
    scanned = call(
        functools.partial(scan_kernel, n_seq),
        in_specs=[VMEM],
        out_specs=VMEM,
        out_shape=shape((2 * width, DH), F32),
        name="scan",
    )(gathered.reshape(2 * width, DH))
    carry = lax.all_to_all(scanned.reshape(n_seq, 1, piece), "seq", 0, 0)
    return call(
        functools.partial(output_kernel, factor),
        in_specs=[VMEM] * 8,
        out_specs=[HBM] * 3,
        out_shape=[shape((tokens, width), BF16)] * 3,
        scratch_shapes=[pltpu.VMEM((tokens, width), BF16)] * 3
        + [pltpu.SemaphoreType.DMA((3, tokens // GROUP, width // DH))],
        name="outputs",
    )(carry.reshape(2 * width, DH), kv0, qg1, *near, g, inner)


def solution(mesh):
    spec = P("seq", "head")
    return jax.shard_map(
        shards,
        mesh=mesh,
        in_specs=(spec,) * 5 + (P("head"),),
        out_specs=(spec,) * 3,
        check_vma=False,
    )
```
